512 devices in a mesh: seq: 16 (over x, y_hi, core), batch: 32 (over z, y_lo).
Axes of the slice: x: 4, y: 4 (y_hi: 2, y_lo: 2; y = y_hi * 2 + y_lo), z: 16, core: 2. Of those that a mesh axis runs over, the one named last changes fastest.
Arguments:
- hidden: bfloat16 [65536, 512], P(('batch', 'seq')), parts along dimension 0, may hold values from -500 to 500
- norm_gain: float32 [512], replicated, may hold values from 0.5 to 1.5
- input_weight: bfloat16 [512, 2176], replicated, may hold values from -0.25 to 0.25
- step_weight: bfloat16 [512, 16], replicated, may hold values from -1 to 1
- conv_weight: float32 [4, 1152], replicated, may hold values from -3 to 3
- conv_bias: float32 [1152], replicated, may hold values from -3 to 3
- step_bias: float32 [16], replicated, may hold values from -11 to 1
- log_rate: float32 [16], replicated, may hold values from -3 to 6
- skip_gain: float32 [16], replicated, may hold values from 0.5 to 1.5
- gate_gain: float32 [1024], replicated, may hold values from 0.5 to 1.5
- output_weight: bfloat16 [1024, 512], replicated, may hold values from -0.1875 to 0.1875
Outputs:
- mixed: bfloat16 [65536, 512], P(('batch', 'seq')), parts along dimension 0
The draws below stay inside these ranges and needn't reach their ends.
There are 32 independent parts, one for each index of `batch`. The reference program is written for one: setup_inputs(seed, part) draws one part's arguments, and reference() takes and returns one part's arrays. A program takes and returns all parts, laid end to end along the dimension named above; an argument that names none is the same for every part. Nothing has to cross between parts.
All inputs are finite; a program needn't handle non-finite values.
Results may differ from the reference program's by a relative error of at most 0.0078.
Values may be sent and summed in bfloat16 or wider, within the bound.
A program may use at most 128 MiB of HBM per device.

```python
import math
import jax
import jax.numpy as jnp
from jax import lax

EMBED_DIM = 512
E = 1024
N = 64
P_SIZE = 64
K = 4
BLOCK = 128
HEADS = 16
TOKEN_COUNT = 2048


def polarity_pattern(feature_count):
    index_row = jnp.arange(feature_count)
    return jnp.where((index_row * 7919 + 13) % 29 < 14, 1.0, -1.0).astype(jnp.float32)


def draw_hidden(key, part):
    prng_seeds = jax.random.split(key, 4)
    drawn_input = jnp.clip(jax.random.normal(prng_seeds[0], (TOKEN_COUNT, EMBED_DIM), jnp.float32), -5.0, 5.0)
    token_multiplier = jnp.exp(jax.random.uniform(prng_seeds[1], (TOKEN_COUNT, 1), jnp.float32) * math.log(10.0))
    channel_multiplier = jnp.exp(jax.random.uniform(prng_seeds[2], (1, EMBED_DIM), jnp.float32) * math.log(10.0))
    spike_input = jax.random.randint(prng_seeds[3], (TOKEN_COUNT, 1), 0, TOKEN_COUNT) < 4
    entry_matrix = jnp.where(spike_input, 8.0 * polarity_pattern(EMBED_DIM)[None, :] + 0.3 * drawn_input, token_multiplier * channel_multiplier * drawn_input)
    return entry_matrix.astype(jnp.bfloat16)


def draw_step_weight(key, part):
    noise = jax.random.normal(key, (EMBED_DIM, HEADS), jnp.float32) / math.sqrt(EMBED_DIM)
    aligned = (math.log(TOKEN_COUNT) + 3.0) * polarity_pattern(EMBED_DIM)[:, None] / EMBED_DIM
    return jnp.clip(noise + aligned, -1.0, 1.0).astype(jnp.bfloat16)


def draw_step_bias(key, part):
    offset = jax.random.uniform(key, (HEADS,), jnp.float32, 0.0, 1.0)
    return (offset - math.log(TOKEN_COUNT)).astype(jnp.float32)


def draw_log_rate(key, part):
    prng_seeds = jax.random.split(key, 3)
    order = jax.random.permutation(prng_seeds[0], HEADS)
    slow = order < HEADS // 2
    slow_value = jax.random.uniform(prng_seeds[1], (HEADS,), jnp.float32, math.log(0.07), math.log(0.25))
    fast_value = jax.random.uniform(prng_seeds[2], (HEADS,), jnp.float32, 0.0, math.log(max(0.013 * TOKEN_COUNT, 2.0)))
    return jnp.where(slow, slow_value, fast_value).astype(jnp.float32)


def bell_draw(stream_key, dims, width, limit, dtype=jnp.bfloat16):
    entries = jax.random.normal(stream_key, dims, jnp.float32) * width
    return jnp.minimum(jnp.maximum(entries, -limit), limit).astype(dtype)


def setup_inputs(seed: int = 0, part: int = 0) -> dict:
    streams_of = jax.random.split(jax.random.key(seed), 12)
    part_splits = jax.random.split(jax.random.fold_in(streams_of[11], part), 12)
    hidden = draw_hidden(jax.random.fold_in(jax.random.fold_in(streams_of[11], part), 71), part)
    norm_gain = jnp.clip(1.0 + 0.1 * jax.random.normal(streams_of[1], (EMBED_DIM,), jnp.float32), 0.5, 1.5)
    input_weight = bell_draw(streams_of[2], (EMBED_DIM, 2 * E + 2 * N), EMBED_DIM ** -0.5, 0.25)
    step_weight = draw_step_weight(jax.random.fold_in(streams_of[11], 71), part)
    conv_weight = bell_draw(streams_of[4], (K, E + 2 * N), K ** -0.5, 3.0, jnp.float32)
    conv_bias = bell_draw(streams_of[5], (E + 2 * N,), 0.5, 3.0, jnp.float32)
    step_bias = draw_step_bias(jax.random.fold_in(streams_of[11], 71), part)
    log_rate = draw_log_rate(jax.random.fold_in(streams_of[11], 71), part)
    skip_gain = jnp.clip(jax.random.uniform(streams_of[8], (HEADS,), jnp.float32, 0.5, 1.5), 0.5, 1.5)
    gate_gain = jnp.clip(1.0 + 0.1 * jax.random.normal(streams_of[9], (E,), jnp.float32), 0.5, 1.5)
    output_weight = bell_draw(streams_of[10], (E, EMBED_DIM), E ** -0.5, 0.1875)
    return dict(hidden=hidden, norm_gain=norm_gain, input_weight=input_weight, step_weight=step_weight, conv_weight=conv_weight, conv_bias=conv_bias, step_bias=step_bias, log_rate=log_rate, skip_gain=skip_gain, gate_gain=gate_gain, output_weight=output_weight)


eps = 1e-05

def normed(entry_matrix, gain):
    floats = entry_matrix.astype(jnp.float32)
    scale = lax.rsqrt(lax.optimization_barrier(jnp.mean(floats * floats, axis=-1, keepdims=True)) + eps)
    return (floats * scale * gain).astype(jnp.bfloat16)

def block_step(memory, pieces):
    signal, writer, reader, log_decay = pieces
    cumulated = jnp.cumsum(log_decay, axis=0)
    per_head = cumulated.T
    spread = per_head[:, :, None] - per_head[:, None, :]
    causal = lax.broadcasted_iota(jnp.int32, (BLOCK, BLOCK), 0) >= lax.broadcasted_iota(jnp.int32, (BLOCK, BLOCK), 1)
    decay = jnp.where(causal[None], jnp.exp(jnp.where(causal[None], spread, 0.0)), 0.0)
    scores = jnp.dot(reader, writer.T, preferred_element_type=jnp.float32)
    weights = (decay * scores[None]).astype(jnp.bfloat16)
    heads_x = signal.reshape(BLOCK, HEADS, P_SIZE)
    inside = jnp.einsum('hts,shp->thp', weights.astype(jnp.float32), heads_x.astype(jnp.float32))
    carried = jnp.einsum('tn,hnp->thp', reader.astype(jnp.float32), memory, precision=lax.Precision.HIGHEST)
    result = inside + jnp.exp(cumulated)[:, :, None] * carried
    decay_tail = jnp.exp(cumulated[-1][None, :] - cumulated)
    decayed = (decay_tail[:, :, None] * heads_x.astype(jnp.float32)).astype(jnp.bfloat16)
    renewed = jnp.exp(cumulated[-1])[:, None, None] * memory + jnp.einsum('sn,shp->hnp', writer.astype(jnp.float32), decayed.astype(jnp.float32))
    return (renewed, result.reshape(BLOCK, E))

def reference(hidden, norm_gain, input_weight, step_weight, conv_weight, conv_bias, step_bias, log_rate, skip_gain, gate_gain, output_weight):

    def mixer(sequence):
        normal_rows = normed(sequence, norm_gain)
        projected = jnp.dot(normal_rows, input_weight, preferred_element_type=jnp.float32).astype(jnp.bfloat16)
        step_raw = jnp.dot(normal_rows, step_weight, preferred_element_type=jnp.float32)
        extended = jnp.concatenate([jnp.zeros((K - 1, E + 2 * N), jnp.bfloat16), projected[:, E:]], axis=0)
        filtered = conv_bias[None, :]
        for tap_index in range(K):
            filtered = filtered + conv_weight[tap_index][None, :] * extended[tap_index:tap_index + TOKEN_COUNT].astype(jnp.float32)
        activated = jax.nn.silu(filtered).astype(jnp.bfloat16)
        signal = activated[:, :E]
        writer = activated[:, E:E + N]
        reader = activated[:, E + N:]
        log_decay = -jnp.exp(log_rate)[None, :] * jax.nn.softplus(step_raw + step_bias[None, :])
        blocks = TOKEN_COUNT // BLOCK
        start = jnp.zeros((HEADS, N, P_SIZE), jnp.float32)
        final_memory, inside = lax.scan(block_step, start, (signal.reshape(blocks, BLOCK, E), writer.reshape(blocks, BLOCK, N), reader.reshape(blocks, BLOCK, N), log_decay.reshape(blocks, BLOCK, HEADS)))
        output_rows = inside.reshape(TOKEN_COUNT, E)
        gated = (output_rows + jnp.repeat(skip_gain, P_SIZE)[None, :] * signal.astype(jnp.float32)) * jax.nn.silu(projected[:, :E].astype(jnp.float32))
        return jnp.dot(normed(gated, gate_gain), output_weight, preferred_element_type=jnp.float32)
    first_chain = mixer(hidden)
    second_chain = mixer(hidden[:, ::-1])
    third_chain = mixer(hidden[::-1])
    fourth_chain = mixer(hidden[::-1, ::-1])
    forward_part = first_chain + second_chain[:, ::-1]
    backward_part = (third_chain + fourth_chain[:, ::-1])[::-1].astype(jnp.bfloat16)
    backward_part = lax.optimization_barrier(backward_part)
    return (forward_part + backward_part.astype(jnp.float32)).astype(jnp.bfloat16)
```

```python
import jax
import jax.numpy as jnp
from jax import lax
from jax.experimental import pallas as pl
from jax.experimental.pallas import tpu as pltpu
from jax.sharding import PartitionSpec as P

D = 512
E = 1024
N = 64
K = 4
BLOCK = 128
HEADS = 16
MIX = E + 2 * N
COUNT = 16
HALO = 16
EPS = 1e-05
LOG2E = 1.4426950408889634

F32 = jnp.float32
BF16 = jnp.bfloat16


def dot(a, b):
    return jnp.dot(a, b, preferred_element_type=F32)


def iota(shape, dim):
    return lax.broadcasted_iota(jnp.int32, shape, dim)


def ones_where(mask):
    return jnp.where(mask, 1.0, 0.0).astype(BF16)


def parts_of(x):
    hi = x.astype(BF16)
    rest = x - hi.astype(F32)
    mid = rest.astype(BF16)
    low = (rest - mid.astype(F32)).astype(BF16)
    return hi, mid, low


def split(x):
    hi, mid, low = parts_of(x)
    group = iota(x.shape, 1) // HEADS
    picked = jnp.where(
        group == 0,
        hi.astype(F32),
        jnp.where(group == 1, mid.astype(F32), jnp.where(group == 2, low.astype(F32), 0.0)),
    )
    return picked.astype(BF16)


def exact(values, ones):
    hi, mid, low = parts_of(values)
    return dot(hi, ones) + dot(mid, ones) + dot(low, ones)


def silu(x):
    return x / (1.0 + jnp.exp(-x))


def kernel(
    hidden,
    norm_gain,
    weight_hbm,
    step_weight,
    conv_weight,
    conv_bias,
    step_bias,
    log_rate,
    skip_gain,
    gate_gain,
    out_weight_hbm,
    out,
    weight,
    out_weight,
    out_flipped,
    halo,
    normal,
    ext,
    act,
    silu_gate,
    inside,
    ecum,
    state_out,
    state_in,
    decay_out,
    decay_in,
    mem_out,
    mem_in,
    expand64,
    expand128,
    load_sem,
    halo_send,
    halo_recv,
    state_send,
    state_recv,
    decay_send,
    decay_recv,
    mem_send,
    mem_recv,
):
    me = lax.axis_index("seq")
    load_w = pltpu.make_async_copy(weight_hbm, weight, load_sem.at[0])
    load_o = pltpu.make_async_copy(out_weight_hbm, out_weight, load_sem.at[1])
    load_w.start()
    load_o.start()

    barrier = pltpu.get_barrier_semaphore()
    for k in range(1, COUNT):
        pl.semaphore_signal(
            barrier,
            inc=1,
            device_id={"seq": lax.rem(me + k, COUNT)},
            device_id_type=pl.DeviceIdType.MESH,
        )

    flip = ones_where(iota((D, D), 0) + iota((D, D), 1) == D - 1)
    rows = iota((BLOCK, E), 0)
    expand64[...] = ones_where((rows % HEADS == iota((BLOCK, E), 1) // 64) & (rows < 3 * HEADS))
    wide = (BLOCK, HEADS * BLOCK)
    rows = iota(wide, 0)
    expand128[...] = ones_where((rows % HEADS == iota(wide, 1) // BLOCK) & (rows < 3 * HEADS))
    tile = ones_where(iota((HEADS, BLOCK), 1) % HEADS == iota((HEADS, BLOCK), 0))
    square = (BLOCK, BLOCK)
    lower = iota(square, 0) >= iota(square, 1)
    upper = iota(square, 0) <= iota(square, 1)
    shift = ones_where(iota(square, 0) == iota(square, 1) + N)
    gain = norm_gain[...]

    def normals(raw):
        floats = raw.astype(F32)
        scale = lax.rsqrt(jnp.mean(floats * floats, axis=-1, keepdims=True) + EPS)
        turned = dot(raw, flip)
        return (floats * scale * gain).astype(BF16), (turned * scale * gain).astype(BF16)

    straight, turned = normals(hidden[...])
    normal[0:BLOCK, :] = straight
    normal[BLOCK : 2 * BLOCK, :] = turned

    step_tiled = dot(step_weight[...], tile).astype(BF16)
    bias = exact(jnp.broadcast_to(step_bias[...], (8, HEADS)), tile)[0:1]
    rate = jnp.exp(exact(jnp.broadcast_to(log_rate[...], (8, HEADS)), tile)[0:1])
    raw = dot(normal[...], step_tiled) + bias
    soft = jnp.maximum(raw, 0.0) + jnp.log1p(jnp.exp(-jnp.abs(raw)))
    log_decay = -rate * soft

    pl.semaphore_wait(barrier, COUNT - 1)
    to_right = pltpu.make_async_remote_copy(
        src_ref=hidden.at[pl.ds(BLOCK - HALO, HALO)],
        dst_ref=halo.at[0],
        send_sem=halo_send.at[0],
        recv_sem=halo_recv.at[0],
        device_id={"seq": lax.rem(me + 1, COUNT)},
        device_id_type=pl.DeviceIdType.MESH,
    )
    to_left = pltpu.make_async_remote_copy(
        src_ref=hidden.at[pl.ds(0, HALO)],
        dst_ref=halo.at[1],
        send_sem=halo_send.at[1],
        recv_sem=halo_recv.at[1],
        device_id={"seq": lax.rem(me + COUNT - 1, COUNT)},
        device_id_type=pl.DeviceIdType.MESH,
    )
    to_right.start()
    to_left.start()

    load_w.wait()
    for c in range(0, MIX, 384):
        cols = slice(c, c + 384)
        mixed = dot(normal[...], weight[:, E + c : E + c + 384]).astype(BF16).astype(F32)
        ext[0, HALO : HALO + BLOCK, cols] = mixed[:BLOCK]
        ext[1, HALO : HALO + BLOCK, cols] = mixed[BLOCK:]

    to_right.wait()
    to_left.wait()
    left_rows = jnp.where(me == 0, 0.0, halo[0].astype(F32))
    right_rows = jnp.where(me == COUNT - 1, 0.0, halo[1].astype(F32))
    rim = jnp.concatenate([left_rows, right_rows], axis=0).astype(BF16)
    rim_normals = jnp.concatenate(normals(rim), axis=0)
    for c in range(0, MIX, 384):
        cols = slice(c, c + 384)
        mixed = dot(rim_normals, weight[:, E + c : E + c + 384]).astype(BF16).astype(F32)
        for j in range(2):
            ext[j, 0:HALO, cols] = mixed[2 * HALO * j : 2 * HALO * j + HALO]
            ext[j, HALO + BLOCK : 2 * HALO + BLOCK, cols] = mixed[
                2 * HALO * j + HALO : 2 * HALO * (j + 1)
            ]

    for c in range(MIX // 128):
        cols = slice(128 * c, 128 * c + 128)
        taps = [conv_weight[k : k + 1, cols] for k in range(K)]
        start = conv_bias[:, cols]
        for j in range(2):
            views = [ext[j, HALO - 3 + r : HALO - 3 + r + BLOCK, cols] for r in range(7)]
            ahead = start
            behind = start
            for k in range(K):
                ahead = ahead + taps[k] * views[k]
                behind = behind + taps[k] * views[6 - k]
            act[j, :, cols] = silu(ahead).astype(BF16)
            act[2 + j, :, cols] = silu(behind).astype(BF16)

    logs = []
    for chain in range(4):
        j, reverse = chain % 2, chain >= 2
        hi, mid, low = parts_of(log_decay[BLOCK * j : BLOCK * (j + 1)])
        tri = ones_where(upper if reverse else lower)
        cumulated = dot(tri, hi) + dot(tri, mid) + dot(tri, low)
        cumulated = cumulated * LOG2E
        last = cumulated[0:1] if reverse else cumulated[BLOCK - 1 : BLOCK]
        logs.append(cumulated)
        if not reverse:
            decay_out[j] = jnp.broadcast_to(jnp.exp2(last), (8, BLOCK))
        tail = split(jnp.exp2(last - cumulated))
        ecum[chain] = split(jnp.exp2(cumulated))
        both = act[chain, :, E:]
        for c in range(0, E, 256):
            cols = slice(c, c + 256)
            factor = dot(tail, expand64[:, cols])
            decayed = (factor * act[chain, :, cols].astype(F32)).astype(BF16)
            state = lax.dot_general(
                both, decayed, (((0,), (0,)), ((), ())), preferred_element_type=F32
            )
            for q in range(4):
                state_out[4 * chain + q, :, cols] = state[16 * q : 16 * q + 16].astype(BF16)

    def state_copy(target, slot):
        return pltpu.make_async_remote_copy(
            src_ref=state_out.at[target],
            dst_ref=state_in.at[slot],
            send_sem=state_send.at[target],
            recv_sem=state_recv.at[slot],
            device_id={"seq": target},
            device_id_type=pl.DeviceIdType.MESH,
        )

    def decay_copy(target, slot):
        return pltpu.make_async_remote_copy(
            src_ref=decay_out.at[lax.rem(target // 4, 2)],
            dst_ref=decay_in.at[slot],
            send_sem=decay_send.at[target],
            recv_sem=decay_recv.at[slot],
            device_id={"seq": target},
            device_id_type=pl.DeviceIdType.MESH,
        )

    def mem_copy(target, slot):
        return pltpu.make_async_remote_copy(
            src_ref=mem_out.at[target],
            dst_ref=mem_in.at[slot],
            send_sem=mem_send.at[target],
            recv_sem=mem_recv.at[slot],
            device_id={"seq": target},
            device_id_type=pl.DeviceIdType.MESH,
        )

    for k in range(1, COUNT):
        target = lax.rem(me + k, COUNT)
        state_copy(target, me).start()
        decay_copy(target, me).start()
    state_in[me] = state_out[me]
    decay_in[me] = decay_out[lax.rem(me // 4, 2)]

    for c in range(0, E, 256):
        cols = slice(c, c + 256)
        gate = dot(normal[...], weight[:, cols]).astype(BF16).astype(F32)
        silu_gate[:, cols] = silu(gate)
    load_o.wait()
    for r in range(0, E, 256):
        out_flipped[r : r + 256, :] = dot(out_weight[r : r + 256, :], flip).astype(BF16)
    repeat = ones_where(iota((HEADS, E), 1) // 64 == iota((HEADS, E), 0))
    skip = exact(jnp.broadcast_to(skip_gain[...], (8, HEADS)), repeat)[0:1]
    first = ones_where(iota(square, 1) < 64)
    second = ones_where(iota(square, 1) >= 64)
    for chain in range(4):
        reverse = chain >= 2
        columns = split(logs[chain])
        by_head = logs[chain].T
        both = act[chain, :, E:]
        reader = dot(both, shift).astype(BF16)
        scores = lax.dot_general(
            reader, both, (((1,), (1,)), ((), ())), preferred_element_type=F32
        )
        scores = jnp.where(upper if reverse else lower, scores, 0.0)
        scores = jnp.concatenate([scores, scores], axis=1)
        for p in range(HEADS // 2):
            cols = slice(128 * p, 128 * p + 128)
            at = dot(columns, expand128[:, 256 * p : 256 * p + 256])
            since = jnp.concatenate(
                [by_head[2 * p : 2 * p + 1], by_head[2 * p + 1 : 2 * p + 2]], axis=1
            )
            weights = (jnp.exp2(jnp.minimum(at - since, 0.0)) * scores).astype(BF16)
            signal = act[chain, :, cols]
            pair = jnp.concatenate([signal * first, signal * second], axis=0)
            inside[chain, :, cols] = dot(weights, pair) + skip[:, cols] * signal.astype(F32)

    onward = me < COUNT // 2
    for k in range(1, COUNT):
        other = lax.rem(me + k, COUNT)
        decay_copy(other, other).wait()
    grouped = decay_in[:, 0, :]
    spread = dot(split(grouped), expand64[...])
    carry = jnp.zeros((16, E), F32)
    for k in range(COUNT):
        source = jnp.where(onward, k, COUNT - 1 - k)
        mem_out[source] = carry.astype(BF16)

        @pl.when(source != me)
        def _():
            state_copy(source, source).wait()
            mem_copy(source, me).start()

        factor = jnp.where(onward, spread[k : k + 1], spread[COUNT - 1 - k : COUNT - k])
        carry = factor * carry + state_in[source].astype(F32)
    mem_in[me] = mem_out[me]
    for k in range(1, COUNT):
        other = lax.rem(me + k, COUNT)
        mem_copy(other, other).wait()

    results = []
    for chain in range(4):
        j = chain % 2
        reader = dot(act[chain, :, E:], shift).astype(BF16)[:, :N]
        memory = mem_in[4 * chain : 4 * chain + 4].reshape(N, E)
        total = jnp.zeros((BLOCK, 1), F32)
        for c in range(0, E, 256):
            cols = slice(c, c + 256)
            carried = dot(reader, memory[:, cols])
            scale = dot(ecum[chain], expand64[:, cols])
            gated = (inside[chain, :, cols] + scale * carried) * silu_gate[
                BLOCK * j : BLOCK * (j + 1), cols
            ]
            total = total + jnp.sum(gated * gated, axis=1, keepdims=True)
            inside[chain, :, cols] = gated
        scale = lax.rsqrt(total / E + EPS)
        final = (inside[chain] * scale * gate_gain[...]).astype(BF16)
        results.append(dot(final, out_weight[...] if j == 0 else out_flipped[...]))
    backward = (results[2] + results[3]).astype(BF16).astype(F32)
    out[...] = (results[0] + results[1] + backward).astype(BF16)


def on_device(
    hidden,
    norm_gain,
    input_weight,
    step_weight,
    conv_weight,
    conv_bias,
    step_bias,
    log_rate,
    skip_gain,
    gate_gain,
    output_weight,
):
    vmem = pl.BlockSpec(memory_space=pltpu.VMEM)
    anywhere = pl.BlockSpec(memory_space=pl.ANY)
    dma = pltpu.SemaphoreType.DMA
    return pl.pallas_call(
        kernel,
        out_shape=jax.ShapeDtypeStruct((BLOCK, D), BF16),
        in_specs=[vmem, vmem, anywhere] + [vmem] * 7 + [anywhere],
        out_specs=vmem,
        scratch_shapes=[
            pltpu.VMEM((D, E + MIX), BF16),
            pltpu.VMEM((E, D), BF16),
            pltpu.VMEM((E, D), BF16),
            pltpu.VMEM((2, HALO, D), BF16),
            pltpu.VMEM((2 * BLOCK, D), BF16),
            pltpu.VMEM((2, BLOCK + 2 * HALO, MIX), F32),
            pltpu.VMEM((4, BLOCK, MIX), BF16),
            pltpu.VMEM((2 * BLOCK, E), F32),
            pltpu.VMEM((4, BLOCK, E), F32),
            pltpu.VMEM((4, BLOCK, BLOCK), BF16),
            pltpu.VMEM((COUNT, 16, E), BF16),
            pltpu.VMEM((COUNT, 16, E), BF16),
            pltpu.VMEM((2, 8, BLOCK), F32),
            pltpu.VMEM((COUNT, 8, BLOCK), F32),
            pltpu.VMEM((COUNT, 16, E), BF16),
            pltpu.VMEM((COUNT, 16, E), BF16),
            pltpu.VMEM((BLOCK, E), BF16),
            pltpu.VMEM((BLOCK, HEADS * BLOCK), BF16),
            dma((2,)),
            dma((2,)),
            dma((2,)),
            dma((COUNT,)),
            dma((COUNT,)),
            dma((COUNT,)),
            dma((COUNT,)),
            dma((COUNT,)),
            dma((COUNT,)),
        ],
        compiler_params=pltpu.CompilerParams(
            collective_id=0, has_side_effects=True, vmem_limit_bytes=48 * 1024 * 1024
        ),
    )(
        hidden,
        norm_gain[None],
        input_weight,
        step_weight,
        conv_weight,
        conv_bias[None],
        step_bias[None],
        log_rate[None],
        skip_gain[None],
        gate_gain[None],
        output_weight,
    )


def solution(mesh):
    in_specs = (P(("batch", "seq"), None), P(), P(), P(), P(), P(), P(), P(), P(), P(), P())
    out_specs = P(("batch", "seq"), None)
    return jax.shard_map(
        on_device, mesh=mesh, in_specs=in_specs, out_specs=out_specs, check_vma=False
    )
```

```python
import jax
import jax.numpy as jnp
from jax import lax
from jax.experimental import pallas as pl
from jax.experimental.pallas import tpu as pltpu
from jax.sharding import PartitionSpec as P

D = 512
E = 1024
N = 64
K = 4
BLOCK = 128
HEADS = 16
MIX = E + 2 * N
COUNT = 16
HALO = 16
EPS = 1e-05
LOG2E = 1.4426950408889634

F32 = jnp.float32
BF16 = jnp.bfloat16


def dot(a, b):
    return jnp.dot(a, b, preferred_element_type=F32)


def iota(shape, dim):
    return lax.broadcasted_iota(jnp.int32, shape, dim)


def ones_where(mask):
    return jnp.where(mask, 1.0, 0.0).astype(BF16)


def parts_of(x):
    hi = x.astype(BF16)
    rest = x - hi.astype(F32)
    mid = rest.astype(BF16)
    low = (rest - mid.astype(F32)).astype(BF16)
    return hi, mid, low


def split(x):
    hi, mid, low = parts_of(x)
    group = iota(x.shape, 1) // HEADS
    picked = jnp.where(
        group == 0,
        hi.astype(F32),
        jnp.where(group == 1, mid.astype(F32), jnp.where(group == 2, low.astype(F32), 0.0)),
    )
    return picked.astype(BF16)


def exact(values, ones):
    hi, mid, low = parts_of(values)
    return dot(hi, ones) + dot(mid, ones) + dot(low, ones)


def silu(x):
    return x / (1.0 + jnp.exp(-x))


def kernel(
    hidden_hbm,
    norm_gain_hbm,
    weight_hbm,
    step_weight_hbm,
    conv_weight_hbm,
    conv_bias_hbm,
    step_bias_hbm,
    log_rate_hbm,
    skip_gain_hbm,
    gate_gain_hbm,
    out_weight_hbm,
    out,
    hidden,
    norm_gain,
    step_weight,
    conv_weight,
    conv_bias,
    step_bias,
    log_rate,
    skip_gain,
    gate_gain,
    weight,
    out_weight,
    out_flipped,
    halo,
    normal,
    ext,
    act,
    silu_gate,
    inside,
    ecum,
    state_out,
    state_in,
    decay_out,
    decay_in,
    mem_out,
    mem_in,
    expand64,
    expand128,
    load_sem,
    halo_send,
    halo_recv,
    state_send,
    state_recv,
    decay_send,
    decay_recv,
    mem_send,
    mem_recv,
):
    me = lax.axis_index("seq")
    moves = [
        (hidden_hbm, hidden),
        (norm_gain_hbm, norm_gain),
        (step_weight_hbm, step_weight),
        (step_bias_hbm, step_bias),
        (log_rate_hbm, log_rate),
        (weight_hbm.at[:, pl.ds(E, MIX)], weight.at[:, pl.ds(E, MIX)]),
        (conv_weight_hbm, conv_weight),
        (conv_bias_hbm, conv_bias),
        (weight_hbm.at[:, pl.ds(0, E)], weight.at[:, pl.ds(0, E)]),
        (skip_gain_hbm, skip_gain),
        (out_weight_hbm, out_weight),
        (gate_gain_hbm, gate_gain),
    ]
    loads = [
        pltpu.make_async_copy(source, target, load_sem.at[i])
        for i, (source, target) in enumerate(moves)
    ]

    barrier = pltpu.get_barrier_semaphore()
    for k in range(1, COUNT):
        pl.semaphore_signal(
            barrier,
            inc=1,
            device_id={"seq": lax.rem(me + k, COUNT)},
            device_id_type=pl.DeviceIdType.MESH,
        )
    for load in loads:
        load.start()

    flip = ones_where(iota((D, D), 0) + iota((D, D), 1) == D - 1)
    rows = iota((BLOCK, E), 0)
    expand64[...] = ones_where((rows % HEADS == iota((BLOCK, E), 1) // 64) & (rows < 3 * HEADS))
    wide = (BLOCK, HEADS * BLOCK)
    rows = iota(wide, 0)
    expand128[...] = ones_where((rows % HEADS == iota(wide, 1) // BLOCK) & (rows < 3 * HEADS))
    tile = ones_where(iota((HEADS, BLOCK), 1) % HEADS == iota((HEADS, BLOCK), 0))
    square = (BLOCK, BLOCK)
    lower = iota(square, 0) >= iota(square, 1)
    upper = iota(square, 0) <= iota(square, 1)
    shift = ones_where(iota(square, 0) == iota(square, 1) + N)
    loads[0].wait()
    loads[1].wait()
    gain = norm_gain[...]

    def normals(raw):
        floats = raw.astype(F32)
        scale = lax.rsqrt(jnp.mean(floats * floats, axis=-1, keepdims=True) + EPS)
        turned = dot(raw, flip)
        return (floats * scale * gain).astype(BF16), (turned * scale * gain).astype(BF16)

    straight, turned = normals(hidden[...])
    normal[0:BLOCK, :] = straight
    normal[BLOCK : 2 * BLOCK, :] = turned

    for load in loads[2:5]:
        load.wait()
    step_tiled = lax.dot_general(
        tile, step_weight[...], (((0,), (0,)), ((), ())), preferred_element_type=F32
    ).astype(BF16)
    bias = exact(jnp.broadcast_to(step_bias[...], (8, HEADS)), tile)[0:1]
    rate = jnp.exp(exact(jnp.broadcast_to(log_rate[...], (8, HEADS)), tile)[0:1])
    raw = bias + lax.dot_general(
        normal[...], step_tiled, (((1,), (1,)), ((), ())), preferred_element_type=F32
    )
    soft = jnp.maximum(raw, 0.0) + jnp.log1p(jnp.exp(-jnp.abs(raw)))
    log_decay = -rate * soft

    pl.semaphore_wait(barrier, COUNT - 1)
    to_right = pltpu.make_async_remote_copy(
        src_ref=hidden.at[pl.ds(BLOCK - HALO, HALO)],
        dst_ref=halo.at[0],
        send_sem=halo_send.at[0],
        recv_sem=halo_recv.at[0],
        device_id={"seq": lax.rem(me + 1, COUNT)},
        device_id_type=pl.DeviceIdType.MESH,
    )
    to_left = pltpu.make_async_remote_copy(
        src_ref=hidden.at[pl.ds(0, HALO)],
        dst_ref=halo.at[1],
        send_sem=halo_send.at[1],
        recv_sem=halo_recv.at[1],
        device_id={"seq": lax.rem(me + COUNT - 1, COUNT)},
        device_id_type=pl.DeviceIdType.MESH,
    )
    to_right.start()
    to_left.start()

    loads[5].wait()
    for c in range(0, MIX, 384):
        cols = slice(c, c + 384)
        mixed = dot(normal[...], weight[:, E + c : E + c + 384]).astype(BF16).astype(F32)
        ext[0, HALO : HALO + BLOCK, cols] = mixed[:BLOCK]
        ext[1, HALO : HALO + BLOCK, cols] = mixed[BLOCK:]

    to_right.wait()
    to_left.wait()
    left_rows = jnp.where(me == 0, 0.0, halo[0].astype(F32))
    right_rows = jnp.where(me == COUNT - 1, 0.0, halo[1].astype(F32))
    rim = jnp.concatenate([left_rows, right_rows], axis=0).astype(BF16)
    rim_normals = jnp.concatenate(normals(rim), axis=0)
    for c in range(0, MIX, 384):
        cols = slice(c, c + 384)
        mixed = dot(rim_normals, weight[:, E + c : E + c + 384]).astype(BF16).astype(F32)
        for j in range(2):
            ext[j, 0:HALO, cols] = mixed[2 * HALO * j : 2 * HALO * j + HALO]
            ext[j, HALO + BLOCK : 2 * HALO + BLOCK, cols] = mixed[
                2 * HALO * j + HALO : 2 * HALO * (j + 1)
            ]

    loads[6].wait()
    loads[7].wait()
    for c in range(MIX // 128):
        cols = slice(128 * c, 128 * c + 128)
        taps = [conv_weight[k : k + 1, cols] for k in range(K)]
        start = conv_bias[cols][None, :]
        for j in range(2):
            views = [ext[j, HALO - 3 + r : HALO - 3 + r + BLOCK, cols] for r in range(7)]
            ahead = start
            behind = start
            for k in range(K):
                ahead = ahead + taps[k] * views[k]
                behind = behind + taps[k] * views[6 - k]
            act[j, :, cols] = silu(ahead).astype(BF16)
            act[2 + j, :, cols] = silu(behind).astype(BF16)

    def state_copy(target, slot):
        return pltpu.make_async_remote_copy(
            src_ref=state_out.at[target],
            dst_ref=state_in.at[slot],
            send_sem=state_send.at[target],
            recv_sem=state_recv.at[slot],
            device_id={"seq": target},
            device_id_type=pl.DeviceIdType.MESH,
        )

    def decay_copy(target, slot):
        return pltpu.make_async_remote_copy(
            src_ref=decay_out.at[lax.rem(target, 2)],
            dst_ref=decay_in.at[slot],
            send_sem=decay_send.at[target],
            recv_sem=decay_recv.at[slot],
            device_id={"seq": target},
            device_id_type=pl.DeviceIdType.MESH,
        )

    def mem_copy(target, slot):
        return pltpu.make_async_remote_copy(
            src_ref=mem_out.at[target],
            dst_ref=mem_in.at[slot],
            send_sem=mem_send.at[target],
            recv_sem=mem_recv.at[slot],
            device_id={"seq": target},
            device_id_type=pl.DeviceIdType.MESH,
        )

    logs = []
    for chain in range(4):
        j, reverse = chain % 2, chain >= 2
        hi, mid, low = parts_of(log_decay[BLOCK * j : BLOCK * (j + 1)])
        tri = ones_where(upper if reverse else lower)
        cumulated = dot(tri, hi) + dot(tri, mid) + dot(tri, low)
        cumulated = cumulated * LOG2E
        last = cumulated[0:1] if reverse else cumulated[BLOCK - 1 : BLOCK]
        logs.append(cumulated)
        if not reverse:
            decay_out[j] = jnp.broadcast_to(jnp.exp2(last), (8, BLOCK))
        tail = split(jnp.exp2(last - cumulated))
        ecum[chain] = split(jnp.exp2(cumulated))
        both = act[chain, :, E:]
        for c in range(0, E, 256):
            cols = slice(c, c + 256)
            factor = dot(tail, expand64[:, cols])
            decayed = (factor * act[chain, :, cols].astype(F32)).astype(BF16)
            state = lax.dot_general(
                both, decayed, (((0,), (0,)), ((), ())), preferred_element_type=F32
            )
            for q in range(4):
                state_out[4 * q + chain, :, cols] = state[16 * q : 16 * q + 16].astype(BF16)
        for q in range(4):
            target = lax.rem(me + 4 * q, COUNT) // 4 * 4 + chain

            @pl.when(target != me)
            def _():
                state_copy(target, me).start()
                decay_copy(target, me).start()

    state_in[me] = state_out[me]
    decay_in[me] = decay_out[lax.rem(me, 2)]

    loads[8].wait()
    for c in range(0, E, 256):
        cols = slice(c, c + 256)
        gate = dot(normal[...], weight[:, cols]).astype(BF16).astype(F32)
        silu_gate[:, cols] = silu(gate)
    loads[9].wait()
    loads[10].wait()
    loads[11].wait()
    for r in range(0, E, 256):
        out_flipped[r : r + 256, :] = dot(out_weight[r : r + 256, :], flip).astype(BF16)
    repeat = ones_where(iota((HEADS, E), 1) // 64 == iota((HEADS, E), 0))
    skip = exact(jnp.broadcast_to(skip_gain[...], (8, HEADS)), repeat)[0:1]
    first = ones_where(iota(square, 1) < 64)
    second = ones_where(iota(square, 1) >= 64)
    for chain in range(4):
        reverse = chain >= 2
        columns = split(logs[chain])
        by_head = logs[chain].T
        both = act[chain, :, E:]
        reader = dot(both, shift).astype(BF16)
        scores = lax.dot_general(
            reader, both, (((1,), (1,)), ((), ())), preferred_element_type=F32
        )
        scores = jnp.where(upper if reverse else lower, scores, 0.0)
        scores = jnp.concatenate([scores, scores], axis=1)
        for p in range(HEADS // 2):
            cols = slice(128 * p, 128 * p + 128)
            at = dot(columns, expand128[:, 256 * p : 256 * p + 256])
            since = jnp.concatenate(
                [by_head[2 * p : 2 * p + 1], by_head[2 * p + 1 : 2 * p + 2]], axis=1
            )
            weights = (jnp.exp2(jnp.minimum(at - since, 0.0)) * scores).astype(BF16)
            signal = act[chain, :, cols]
            pair = jnp.concatenate([signal * first, signal * second], axis=0)
            inside[chain, :, cols] = dot(weights, pair) + skip[:, cols] * signal.astype(F32)

    onward = lax.rem(me, 4) < 2
    for k in range(1, COUNT):
        other = lax.rem(me + k, COUNT)
        decay_copy(other, other).wait()
    grouped = decay_in[:, 0, :]
    spread = dot(split(grouped), expand64[...])
    carry = jnp.zeros((16, E), F32)
    for k in range(COUNT):
        source = jnp.where(onward, k, COUNT - 1 - k)
        mem_out[source] = carry.astype(BF16)

        @pl.when(source != me)
        def _():
            state_copy(source, source).wait()
            mem_copy(source, me).start()

        factor = jnp.where(onward, spread[k : k + 1], spread[COUNT - 1 - k : COUNT - k])
        carry = factor * carry + state_in[source].astype(F32)
    mem_in[me] = mem_out[me]
    results = []
    for chain in range(4):
        j = chain % 2
        for q in range(4):
            owner = 4 * q + chain

            @pl.when(owner != me)
            def _():
                mem_copy(owner, owner).wait()

        reader = dot(act[chain, :, E:], shift).astype(BF16)[:, :N]
        memory = jnp.concatenate([mem_in[4 * q + chain] for q in range(4)], axis=0)
        total = jnp.zeros((BLOCK, 1), F32)
        for c in range(0, E, 256):
            cols = slice(c, c + 256)
            carried = dot(reader, memory[:, cols])
            scale = dot(ecum[chain], expand64[:, cols])
            gated = (inside[chain, :, cols] + scale * carried) * silu_gate[
                BLOCK * j : BLOCK * (j + 1), cols
            ]
            total = total + jnp.sum(gated * gated, axis=1, keepdims=True)
            inside[chain, :, cols] = gated
        scale = lax.rsqrt(total / E + EPS)
        final = (inside[chain] * scale * gate_gain[...]).astype(BF16)
        results.append(dot(final, out_weight[...] if j == 0 else out_flipped[...]))
    backward = (results[2] + results[3]).astype(BF16).astype(F32)
    out[...] = (results[0] + results[1] + backward).astype(BF16)


def on_device(
    hidden,
    norm_gain,
    input_weight,
    step_weight,
    conv_weight,
    conv_bias,
    step_bias,
    log_rate,
    skip_gain,
    gate_gain,
    output_weight,
):
    vmem = pl.BlockSpec(memory_space=pltpu.VMEM)
    dma = pltpu.SemaphoreType.DMA
    return pl.pallas_call(
        kernel,
        out_shape=jax.ShapeDtypeStruct((BLOCK, D), BF16),
        in_specs=[pl.BlockSpec(memory_space=pltpu.HBM)] * 11,
        out_specs=vmem,
        scratch_shapes=[
            pltpu.VMEM((BLOCK, D), BF16),
            pltpu.VMEM((1, D), F32),
            pltpu.VMEM((HEADS, D), BF16),
            pltpu.VMEM((K, MIX), F32),
            pltpu.VMEM((MIX,), F32),
            pltpu.VMEM((1, HEADS), F32),
            pltpu.VMEM((1, HEADS), F32),
            pltpu.VMEM((1, HEADS), F32),
            pltpu.VMEM((1, E), F32),
            pltpu.VMEM((D, E + MIX), BF16),
            pltpu.VMEM((E, D), BF16),
            pltpu.VMEM((E, D), BF16),
            pltpu.VMEM((2, HALO, D), BF16),
            pltpu.VMEM((2 * BLOCK, D), BF16),
            pltpu.VMEM((2, BLOCK + 2 * HALO, MIX), F32),
            pltpu.VMEM((4, BLOCK, MIX), BF16),
            pltpu.VMEM((2 * BLOCK, E), F32),
            pltpu.VMEM((4, BLOCK, E), F32),
            pltpu.VMEM((4, BLOCK, BLOCK), BF16),
            pltpu.VMEM((COUNT, 16, E), BF16),
            pltpu.VMEM((COUNT, 16, E), BF16),
            pltpu.VMEM((2, 8, BLOCK), F32),
            pltpu.VMEM((COUNT, 8, BLOCK), F32),
            pltpu.VMEM((COUNT, 16, E), BF16),
            pltpu.VMEM((COUNT, 16, E), BF16),
            pltpu.VMEM((BLOCK, E), BF16),
            pltpu.VMEM((BLOCK, HEADS * BLOCK), BF16),
            dma((12,)),
            dma((2,)),
            dma((2,)),
            dma((COUNT,)),
            dma((COUNT,)),
            dma((COUNT,)),
            dma((COUNT,)),
            dma((COUNT,)),
            dma((COUNT,)),
        ],
        compiler_params=pltpu.CompilerParams(
            collective_id=0, has_side_effects=True, vmem_limit_bytes=60 * 1024 * 1024
        ),
    )(
        hidden,
        norm_gain[None],
        input_weight,
        step_weight.T,
        conv_weight,
        conv_bias,
        step_bias[None],
        log_rate[None],
        skip_gain[None],
        gate_gain[None],
        output_weight,
    )


def solution(mesh):
    in_specs = (P(("batch", "seq"), None), P(), P(), P(), P(), P(), P(), P(), P(), P(), P())
    out_specs = P(("batch", "seq"), None)
    return jax.shard_map(
        on_device, mesh=mesh, in_specs=in_specs, out_specs=out_specs, check_vma=False
    )
```

```python
import jax
import jax.numpy as jnp
from jax import lax
from jax.experimental import pallas as pl
from jax.experimental.pallas import tpu as pltpu
from jax.sharding import PartitionSpec as P

D = 512
E = 1024
N = 64
K = 4
BLOCK = 128
HEADS = 16
MIX = E + 2 * N
COUNT = 16
HALO = 16
EPS = 1e-05
LOG2E = 1.4426950408889634

F32 = jnp.float32
BF16 = jnp.bfloat16


def dot(a, b):
    return jnp.dot(a, b, preferred_element_type=F32)


def iota(shape, dim):
    return lax.broadcasted_iota(jnp.int32, shape, dim)


def ones_where(mask):
    return jnp.where(mask, 1.0, 0.0).astype(BF16)


def parts_of(x):
    hi = x.astype(BF16)
    rest = x - hi.astype(F32)
    mid = rest.astype(BF16)
    low = (rest - mid.astype(F32)).astype(BF16)
    return hi, mid, low


def split(x):
    hi, mid, low = parts_of(x)
    group = iota(x.shape, 1) // HEADS
    picked = jnp.where(
        group == 0,
        hi.astype(F32),
        jnp.where(group == 1, mid.astype(F32), jnp.where(group == 2, low.astype(F32), 0.0)),
    )
    return picked.astype(BF16)


def exact(values, ones):
    hi, mid, low = parts_of(values)
    return dot(hi, ones) + dot(mid, ones) + dot(low, ones)


def silu(x):
    return x / (1.0 + jnp.exp(-x))


def kernel(
    hidden_hbm,
    norm_gain_hbm,
    weight_hbm,
    step_weight_hbm,
    conv_weight_hbm,
    conv_bias_hbm,
    step_bias_hbm,
    log_rate_hbm,
    skip_gain_hbm,
    gate_gain_hbm,
    out_weight_hbm,
    out,
    hidden,
    norm_gain,
    step_weight,
    conv_weight,
    conv_bias,
    step_bias,
    log_rate,
    skip_gain,
    gate_gain,
    weight,
    out_weight,
    out_flipped,
    halo,
    normal,
    ext,
    act,
    silu_gate,
    inside,
    ecum,
    tails,
    cums,
    pair_out,
    pair_in,
    decay_out,
    decay_in,
    sum_out,
    sum_in,
    mem_out,
    mem_in,
    cross_out,
    cross_in,
    expand64,
    expand128,
    load_sem,
    halo_send,
    halo_recv,
    decay_send,
    decay_recv,
    pair_send,
    pair_recv,
    sum_send,
    sum_recv,
    mem_send,
    mem_recv,
    cross_send,
    cross_recv,
):
    me = lax.axis_index("seq")
    chip, core = me // 2, lax.rem(me, 2)
    partner = me + 1 - 2 * core
    moves = [
        (hidden_hbm, hidden),
        (norm_gain_hbm, norm_gain),
        (step_weight_hbm, step_weight),
        (step_bias_hbm, step_bias),
        (log_rate_hbm, log_rate),
        (weight_hbm.at[:, pl.ds(E, MIX)], weight.at[:, pl.ds(E, MIX)]),
        (conv_weight_hbm, conv_weight),
        (conv_bias_hbm, conv_bias),
        (weight_hbm.at[:, pl.ds(0, E)], weight.at[:, pl.ds(0, E)]),
        (skip_gain_hbm, skip_gain),
        (out_weight_hbm, out_weight),
        (gate_gain_hbm, gate_gain),
    ]
    loads = [
        pltpu.make_async_copy(source, target, load_sem.at[i])
        for i, (source, target) in enumerate(moves)
    ]

    barrier = pltpu.get_barrier_semaphore()
    for k in range(1, COUNT):
        pl.semaphore_signal(
            barrier,
            inc=1,
            device_id={"seq": lax.rem(me + k, COUNT)},
            device_id_type=pl.DeviceIdType.MESH,
        )
    for load in loads:
        load.start()

    flip = ones_where(iota((D, D), 0) + iota((D, D), 1) == D - 1)
    rows = iota((BLOCK, E), 0)
    expand64[...] = ones_where((rows % HEADS == iota((BLOCK, E), 1) // 64) & (rows < 3 * HEADS))
    wide = (BLOCK, HEADS * BLOCK)
    rows = iota(wide, 0)
    expand128[...] = ones_where((rows % HEADS == iota(wide, 1) // BLOCK) & (rows < 3 * HEADS))
    tile = ones_where(iota((HEADS, BLOCK), 1) % HEADS == iota((HEADS, BLOCK), 0))
    square = (BLOCK, BLOCK)
    lower = iota(square, 0) >= iota(square, 1)
    upper = iota(square, 0) <= iota(square, 1)
    shift = ones_where(iota(square, 0) == iota(square, 1) + N)
    loads[0].wait()
    loads[1].wait()
    gain = norm_gain[...]

    def normals(raw):
        floats = raw.astype(F32)
        scale = lax.rsqrt(jnp.mean(floats * floats, axis=-1, keepdims=True) + EPS)
        turned = dot(raw, flip)
        return (floats * scale * gain).astype(BF16), (turned * scale * gain).astype(BF16)

    straight, turned = normals(hidden[...])
    normal[0:BLOCK, :] = straight
    normal[BLOCK : 2 * BLOCK, :] = turned

    for load in loads[2:5]:
        load.wait()
    step_tiled = lax.dot_general(
        tile, step_weight[...], (((0,), (0,)), ((), ())), preferred_element_type=F32
    ).astype(BF16)
    bias = exact(jnp.broadcast_to(step_bias[...], (8, HEADS)), tile)[0:1]
    rate = jnp.exp(exact(jnp.broadcast_to(log_rate[...], (8, HEADS)), tile)[0:1])
    raw = bias + lax.dot_general(
        normal[...], step_tiled, (((1,), (1,)), ((), ())), preferred_element_type=F32
    )
    soft = jnp.maximum(raw, 0.0) + jnp.log1p(jnp.exp(-jnp.abs(raw)))
    log_decay = -rate * soft
    lasts = []
    for chain in range(4):
        j, reverse = chain % 2, chain >= 2
        hi, mid, low = parts_of(log_decay[BLOCK * j : BLOCK * (j + 1)])
        tri = ones_where(upper if reverse else lower)
        cumulated = (dot(tri, hi) + dot(tri, mid) + dot(tri, low)) * LOG2E
        last = cumulated[0:1] if reverse else cumulated[BLOCK - 1 : BLOCK]
        if not reverse:
            lasts.append(jnp.exp2(last))
        cums[chain] = cumulated
        tails[chain] = split(jnp.exp2(last - cumulated))
        ecum[chain] = split(jnp.exp2(cumulated))
    top = iota((8, BLOCK), 0) == 0
    decays = jnp.where(top, lasts[0], lasts[1])
    decay_out[...] = decays
    decay_in[me] = decays

    pl.semaphore_wait(barrier, COUNT - 1)
    to_right = pltpu.make_async_remote_copy(
        src_ref=hidden.at[pl.ds(BLOCK - HALO, HALO)],
        dst_ref=halo.at[0],
        send_sem=halo_send.at[0],
        recv_sem=halo_recv.at[0],
        device_id={"seq": lax.rem(me + 1, COUNT)},
        device_id_type=pl.DeviceIdType.MESH,
    )
    to_left = pltpu.make_async_remote_copy(
        src_ref=hidden.at[pl.ds(0, HALO)],
        dst_ref=halo.at[1],
        send_sem=halo_send.at[1],
        recv_sem=halo_recv.at[1],
        device_id={"seq": lax.rem(me + COUNT - 1, COUNT)},
        device_id_type=pl.DeviceIdType.MESH,
    )
    to_right.start()
    to_left.start()

    def decay_copy(target, slot):
        return pltpu.make_async_remote_copy(
            src_ref=decay_out,
            dst_ref=decay_in.at[slot],
            send_sem=decay_send.at[target],
            recv_sem=decay_recv.at[slot],
            device_id={"seq": target},
            device_id_type=pl.DeviceIdType.MESH,
        )

    def pair_copy(j):
        return pltpu.make_async_remote_copy(
            src_ref=pair_out.at[2 * (1 - core) + j],
            dst_ref=pair_in.at[j],
            send_sem=pair_send.at[j],
            recv_sem=pair_recv.at[j],
            device_id={"seq": partner},
            device_id_type=pl.DeviceIdType.MESH,
        )

    def sum_copy(target, slot):
        return pltpu.make_async_remote_copy(
            src_ref=sum_out.at[target],
            dst_ref=sum_in.at[slot],
            send_sem=sum_send.at[target],
            recv_sem=sum_recv.at[slot],
            device_id={"seq": 2 * target + core},
            device_id_type=pl.DeviceIdType.MESH,
        )

    def mem_copy(target, slot):
        return pltpu.make_async_remote_copy(
            src_ref=mem_out.at[target],
            dst_ref=mem_in.at[slot],
            send_sem=mem_send.at[target],
            recv_sem=mem_recv.at[slot],
            device_id={"seq": 2 * target + core},
            device_id_type=pl.DeviceIdType.MESH,
        )

    def cross_copy(j):
        return pltpu.make_async_remote_copy(
            src_ref=cross_out.at[j],
            dst_ref=cross_in.at[j],
            send_sem=cross_send.at[j],
            recv_sem=cross_recv.at[j],
            device_id={"seq": partner},
            device_id_type=pl.DeviceIdType.MESH,
        )

    for k in range(1, COUNT):
        decay_copy(lax.rem(me + k, COUNT), me).start()

    loads[5].wait()
    for c in range(0, MIX, 384):
        cols = slice(c, c + 384)
        mixed = dot(normal[...], weight[:, E + c : E + c + 384]).astype(BF16).astype(F32)
        ext[0, HALO : HALO + BLOCK, cols] = mixed[:BLOCK]
        ext[1, HALO : HALO + BLOCK, cols] = mixed[BLOCK:]

    to_right.wait()
    to_left.wait()
    left_rows = jnp.where(me == 0, 0.0, halo[0].astype(F32))
    right_rows = jnp.where(me == COUNT - 1, 0.0, halo[1].astype(F32))
    rim = jnp.concatenate([left_rows, right_rows], axis=0).astype(BF16)
    rim_normals = jnp.concatenate(normals(rim), axis=0)
    for c in range(0, MIX, 384):
        cols = slice(c, c + 384)
        mixed = dot(rim_normals, weight[:, E + c : E + c + 384]).astype(BF16).astype(F32)
        for j in range(2):
            ext[j, 0:HALO, cols] = mixed[2 * HALO * j : 2 * HALO * j + HALO]
            ext[j, HALO + BLOCK : 2 * HALO + BLOCK, cols] = mixed[
                2 * HALO * j + HALO : 2 * HALO * (j + 1)
            ]

    loads[6].wait()
    loads[7].wait()
    for c in range(MIX // 128):
        cols = slice(128 * c, 128 * c + 128)
        taps = [conv_weight[k : k + 1, cols] for k in range(K)]
        start = conv_bias[cols][None, :]
        for j in range(2):
            views = [ext[j, HALO - 3 + r : HALO - 3 + r + BLOCK, cols] for r in range(7)]
            ahead = start
            behind = start
            for k in range(K):
                ahead = ahead + taps[k] * views[k]
                behind = behind + taps[k] * views[6 - k]
            act[j, :, cols] = silu(ahead).astype(BF16)
            act[2 + j, :, cols] = silu(behind).astype(BF16)

    for chain, j in [(2 * (1 - core) + j, j) for j in range(2)] + [(2 * core + j, None) for j in range(2)]:
        both = act[chain, :, E:]
        for c in range(0, E, 256):
            cols = slice(c, c + 256)
            factor = dot(tails[chain], expand64[:, cols])
            decayed = (factor * act[chain, :, cols].astype(F32)).astype(BF16)
            state = lax.dot_general(
                both, decayed, (((0,), (0,)), ((), ())), preferred_element_type=F32
            )
            pair_out[chain, :, cols] = state[:N].astype(BF16)
        if j is not None:
            pair_copy(j).start()

    for k in range(1, COUNT):
        other = lax.rem(me + k, COUNT)
        decay_copy(other, other).wait()
    near = [dot(split(decay_in[d]), expand64[...]) for d in (me, partner)]
    for j in range(2):
        pair_copy(j).wait()
        joined = near[1][j : j + 1] * pair_out[2 * core + j].astype(F32) + pair_in[j].astype(F32)
        joined = joined.astype(BF16)
        for q in range(4):
            sum_out[4 * j + q] = joined[16 * q : 16 * q + 16]
        for q in range(4):
            target = 4 * j + lax.rem(chip + q, 4)

            @pl.when(target != chip)
            def _():
                sum_copy(target, chip).start()
    sum_in[chip] = sum_out[chip]

    loads[8].wait()
    for c in range(0, E, 256):
        cols = slice(c, c + 256)
        gate = dot(normal[...], weight[:, cols]).astype(BF16).astype(F32)
        silu_gate[:, cols] = silu(gate)
    loads[9].wait()
    loads[10].wait()
    loads[11].wait()
    for r in range(0, E, 256):
        out_flipped[r : r + 256, :] = dot(out_weight[r : r + 256, :], flip).astype(BF16)
    repeat = ones_where(iota((HEADS, E), 1) // 64 == iota((HEADS, E), 0))
    skip = exact(jnp.broadcast_to(skip_gain[...], (8, HEADS)), repeat)[0:1]
    first = ones_where(iota(square, 1) < 64)
    second = ones_where(iota(square, 1) >= 64)
    for chain in range(4):
        reverse = chain >= 2
        columns = split(cums[chain])
        by_head = cums[chain].T
        both = act[chain, :, E:]
        reader = dot(both, shift).astype(BF16)
        scores = lax.dot_general(
            reader, both, (((1,), (1,)), ((), ())), preferred_element_type=F32
        )
        scores = jnp.where(upper if reverse else lower, scores, 0.0)
        scores = jnp.concatenate([scores, scores], axis=1)
        for p in range(HEADS // 2):
            cols = slice(128 * p, 128 * p + 128)
            at = dot(columns, expand128[:, 256 * p : 256 * p + 256])
            since = jnp.concatenate(
                [by_head[2 * p : 2 * p + 1], by_head[2 * p + 1 : 2 * p + 2]], axis=1
            )
            weights = (jnp.exp2(jnp.minimum(at - since, 0.0)) * scores).astype(BF16)
            signal = act[chain, :, cols]
            pair = jnp.concatenate([signal * first, signal * second], axis=0)
            inside[chain, :, cols] = dot(weights, pair) + skip[:, cols] * signal.astype(F32)

    mine = jnp.where(chip < 4, decay_in[:, 0, :], decay_in[:, 1, :])
    spread = dot(split(mine), expand64[...])
    carry = jnp.zeros((16, E), F32)
    for k in range(COUNT // 2):
        back = COUNT // 2 - 1 - k
        source = jnp.where(core == 0, k, back)
        mem_out[source] = carry.astype(BF16)

        @pl.when(source != chip)
        def _():
            sum_copy(source, source).wait()
            mem_copy(source, chip).start()

        factor = jnp.where(
            core == 0,
            spread[2 * k : 2 * k + 1] * spread[2 * k + 1 : 2 * k + 2],
            spread[2 * back : 2 * back + 1] * spread[2 * back + 1 : 2 * back + 2],
        )
        carry = factor * carry + sum_in[source].astype(F32)
    mem_in[chip] = mem_out[chip]

    def finish(chain, j, memory):
        reader = dot(act[chain, :, E:], shift).astype(BF16)[:, :N]
        total = jnp.zeros((BLOCK, 1), F32)
        for c in range(0, E, 256):
            cols = slice(c, c + 256)
            carried = dot(reader, memory[:, cols])
            scale = dot(ecum[chain], expand64[:, cols])
            gated = (inside[chain, :, cols] + scale * carried) * silu_gate[
                BLOCK * j : BLOCK * (j + 1), cols
            ]
            total = total + jnp.sum(gated * gated, axis=1, keepdims=True)
            inside[chain, :, cols] = gated
        scale = lax.rsqrt(total / E + EPS)
        final = (inside[chain] * scale * gate_gain[...]).astype(BF16)
        return dot(final, out_weight[...] if j == 0 else out_flipped[...])

    memories = []
    for j in range(2):
        for q in range(4):
            owner = 4 * j + q

            @pl.when(owner != chip)
            def _():
                mem_copy(owner, owner).wait()

        memory = jnp.concatenate([mem_in[4 * j + q] for q in range(4)], axis=0)
        onward = near[0][j : j + 1] * memory.astype(F32) + pair_out[2 * core + j].astype(F32)
        cross_out[j] = onward.astype(BF16)
        cross_copy(j).start()
        memories.append(memory)
    own = finish(2 * core, 0, memories[0]) + finish(2 * core + 1, 1, memories[1])
    other = jnp.zeros((BLOCK, D), F32)
    for j in range(2):
        cross_copy(j).wait()
        other = other + finish(2 * (1 - core) + j, j, cross_in[j])
    forward = jnp.where(core == 0, own, other)
    backward = jnp.where(core == 0, other, own).astype(BF16).astype(F32)
    out[...] = (forward + backward).astype(BF16)


def on_device(
    hidden,
    norm_gain,
    input_weight,
    step_weight,
    conv_weight,
    conv_bias,
    step_bias,
    log_rate,
    skip_gain,
    gate_gain,
    output_weight,
):
    vmem = pl.BlockSpec(memory_space=pltpu.VMEM)
    dma = pltpu.SemaphoreType.DMA
    return pl.pallas_call(
        kernel,
        out_shape=jax.ShapeDtypeStruct((BLOCK, D), BF16),
        in_specs=[pl.BlockSpec(memory_space=pltpu.HBM)] * 11,
        out_specs=vmem,
        scratch_shapes=[
            pltpu.VMEM((BLOCK, D), BF16),
            pltpu.VMEM((1, D), F32),
            pltpu.VMEM((HEADS, D), BF16),
            pltpu.VMEM((K, MIX), F32),
            pltpu.VMEM((MIX,), F32),
            pltpu.VMEM((1, HEADS), F32),
            pltpu.VMEM((1, HEADS), F32),
            pltpu.VMEM((1, HEADS), F32),
            pltpu.VMEM((1, E), F32),
            pltpu.VMEM((D, E + MIX), BF16),
            pltpu.VMEM((E, D), BF16),
            pltpu.VMEM((E, D), BF16),
            pltpu.VMEM((2, HALO, D), BF16),
            pltpu.VMEM((2 * BLOCK, D), BF16),
            pltpu.VMEM((2, BLOCK + 2 * HALO, MIX), F32),
            pltpu.VMEM((4, BLOCK, MIX), BF16),
            pltpu.VMEM((2 * BLOCK, E), F32),
            pltpu.VMEM((4, BLOCK, E), F32),
            pltpu.VMEM((4, BLOCK, BLOCK), BF16),
            pltpu.VMEM((4, BLOCK, BLOCK), BF16),
            pltpu.VMEM((4, BLOCK, BLOCK), F32),
            pltpu.VMEM((4, N, E), BF16),
            pltpu.VMEM((2, N, E), BF16),
            pltpu.VMEM((8, BLOCK), F32),
            pltpu.VMEM((COUNT, 8, BLOCK), F32),
            pltpu.VMEM((COUNT // 2, 16, E), BF16),
            pltpu.VMEM((COUNT // 2, 16, E), BF16),
            pltpu.VMEM((COUNT // 2, 16, E), BF16),
            pltpu.VMEM((COUNT // 2, 16, E), BF16),
            pltpu.VMEM((2, N, E), BF16),
            pltpu.VMEM((2, N, E), BF16),
            pltpu.VMEM((BLOCK, E), BF16),
            pltpu.VMEM((BLOCK, HEADS * BLOCK), BF16),
            dma((12,)),
            dma((2,)),
            dma((2,)),
            dma((COUNT,)),
            dma((COUNT,)),
            dma((2,)),
            dma((2,)),
            dma((COUNT // 2,)),
            dma((COUNT // 2,)),
            dma((COUNT // 2,)),
            dma((COUNT // 2,)),
            dma((2,)),
            dma((2,)),
        ],
        compiler_params=pltpu.CompilerParams(
            collective_id=0, has_side_effects=True, vmem_limit_bytes=60 * 1024 * 1024
        ),
    )(
        hidden,
        norm_gain[None],
        input_weight,
        step_weight.T,
        conv_weight,
        conv_bias,
        step_bias[None],
        log_rate[None],
        skip_gain[None],
        gate_gain[None],
        output_weight,
    )


def solution(mesh):
    in_specs = (P(("batch", "seq"), None), P(), P(), P(), P(), P(), P(), P(), P(), P(), P())
    out_specs = P(("batch", "seq"), None)
    return jax.shard_map(
        on_device, mesh=mesh, in_specs=in_specs, out_specs=out_specs, check_vma=False
    )
```

```python
import jax
import jax.numpy as jnp
from jax import lax
from jax.experimental import pallas as pl
from jax.experimental.pallas import tpu as pltpu
from jax.sharding import PartitionSpec as P

D = 512
E = 1024
N = 64
K = 4
BLOCK = 128
HEADS = 16
MIX = E + 2 * N
COUNT = 16
HALO = 16
EPS = 1e-05
LOG2E = 1.4426950408889634

F32 = jnp.float32
BF16 = jnp.bfloat16


def dot(a, b):
    return jnp.dot(a, b, preferred_element_type=F32)


def iota(shape, dim):
    return lax.broadcasted_iota(jnp.int32, shape, dim)


def ones_where(mask):
    return jnp.where(mask, 1.0, 0.0).astype(BF16)


def parts_of(x):
    hi = x.astype(BF16)
    rest = x - hi.astype(F32)
    mid = rest.astype(BF16)
    low = (rest - mid.astype(F32)).astype(BF16)
    return hi, mid, low


def split(x):
    hi, mid, low = parts_of(x)
    group = iota(x.shape, 1) // HEADS
    picked = jnp.where(
        group == 0,
        hi.astype(F32),
        jnp.where(group == 1, mid.astype(F32), jnp.where(group == 2, low.astype(F32), 0.0)),
    )
    return picked.astype(BF16)


def exact(values, ones):
    hi, mid, low = parts_of(values)
    return dot(hi, ones) + dot(mid, ones) + dot(low, ones)


def silu(x):
    return x / (1.0 + jnp.exp(-x))


def kernel(
    hidden_hbm,
    norm_gain_hbm,
    weight_hbm,
    step_weight_hbm,
    conv_weight_hbm,
    conv_bias_hbm,
    step_bias_hbm,
    log_rate_hbm,
    skip_gain_hbm,
    gate_gain_hbm,
    out_weight_hbm,
    out,
    hidden,
    norm_gain,
    step_weight,
    conv_weight,
    conv_bias,
    step_bias,
    log_rate,
    skip_gain,
    gate_gain,
    weight,
    out_weight,
    out_flipped,
    halo,
    normal,
    ext,
    act,
    silu_gate,
    inside,
    ecum,
    tails,
    cums,
    pair_out,
    pair_in,
    decay_out,
    decay_in,
    sum_out,
    sum_in,
    mem_out,
    mem_in,
    cross_out,
    cross_in,
    expand64,
    expand128,
    load_sem,
    halo_send,
    halo_recv,
    decay_send,
    decay_recv,
    pair_send,
    pair_recv,
    sum_send,
    sum_recv,
    mem_send,
    mem_recv,
    cross_send,
    cross_recv,
):
    me = lax.axis_index("seq")
    chip, core = me // 2, lax.rem(me, 2)
    partner = me + 1 - 2 * core
    moves = [
        (hidden_hbm, hidden),
        (norm_gain_hbm, norm_gain),
        (step_weight_hbm, step_weight),
        (step_bias_hbm, step_bias),
        (log_rate_hbm, log_rate),
        (weight_hbm.at[:, pl.ds(E, MIX)], weight.at[:, pl.ds(E, MIX)]),
        (conv_weight_hbm, conv_weight),
        (conv_bias_hbm, conv_bias),
        (weight_hbm.at[:, pl.ds(0, E)], weight.at[:, pl.ds(0, E)]),
        (skip_gain_hbm, skip_gain),
        (out_weight_hbm, out_weight),
        (gate_gain_hbm, gate_gain),
    ]
    loads = [
        pltpu.make_async_copy(source, target, load_sem.at[i])
        for i, (source, target) in enumerate(moves)
    ]

    loads[0].start()
    barrier = pltpu.get_barrier_semaphore()
    for k in range(1, COUNT):
        pl.semaphore_signal(
            barrier,
            inc=1,
            device_id={"seq": lax.rem(me + k, COUNT)},
            device_id_type=pl.DeviceIdType.MESH,
        )
    for load in loads[1:]:
        load.start()

    flip = ones_where(iota((D, D), 0) + iota((D, D), 1) == D - 1)
    rows = iota((BLOCK, E), 0)
    expand64[...] = ones_where((rows % HEADS == iota((BLOCK, E), 1) // 64) & (rows < 3 * HEADS))
    wide = (BLOCK, HEADS * BLOCK)
    rows = iota(wide, 0)
    expand128[...] = ones_where((rows % HEADS == iota(wide, 1) // BLOCK) & (rows < 3 * HEADS))
    tile = ones_where(iota((HEADS, BLOCK), 1) % HEADS == iota((HEADS, BLOCK), 0))
    square = (BLOCK, BLOCK)
    lower = iota(square, 0) >= iota(square, 1)
    upper = iota(square, 0) <= iota(square, 1)
    shift = ones_where(iota(square, 0) == iota(square, 1) + N)
    loads[0].wait()
    pl.semaphore_wait(barrier, COUNT - 1)
    to_right = pltpu.make_async_remote_copy(
        src_ref=hidden.at[pl.ds(BLOCK - HALO, HALO)],
        dst_ref=halo.at[0],
        send_sem=halo_send.at[0],
        recv_sem=halo_recv.at[0],
        device_id={"seq": lax.rem(me + 1, COUNT)},
        device_id_type=pl.DeviceIdType.MESH,
    )
    to_left = pltpu.make_async_remote_copy(
        src_ref=hidden.at[pl.ds(0, HALO)],
        dst_ref=halo.at[1],
        send_sem=halo_send.at[1],
        recv_sem=halo_recv.at[1],
        device_id={"seq": lax.rem(me + COUNT - 1, COUNT)},
        device_id_type=pl.DeviceIdType.MESH,
    )
    to_right.start()
    to_left.start()

    loads[1].wait()
    gain = norm_gain[...]

    def normals(raw):
        floats = raw.astype(F32)
        scale = lax.rsqrt(jnp.mean(floats * floats, axis=-1, keepdims=True) + EPS)
        turned = dot(raw, flip)
        return (floats * scale * gain).astype(BF16), (turned * scale * gain).astype(BF16)

    straight, turned = normals(hidden[...])
    normal[0:BLOCK, :] = straight
    normal[BLOCK : 2 * BLOCK, :] = turned

    for load in loads[2:5]:
        load.wait()
    step_tiled = lax.dot_general(
        tile, step_weight[...], (((0,), (0,)), ((), ())), preferred_element_type=F32
    ).astype(BF16)
    bias = exact(jnp.broadcast_to(step_bias[...], (8, HEADS)), tile)[0:1]
    rate = jnp.exp(exact(jnp.broadcast_to(log_rate[...], (8, HEADS)), tile)[0:1])
    raw = bias + lax.dot_general(
        normal[...], step_tiled, (((1,), (1,)), ((), ())), preferred_element_type=F32
    )
    soft = jnp.maximum(raw, 0.0) + jnp.log1p(jnp.exp(-jnp.abs(raw)))
    log_decay = -rate * soft
    lasts = []
    for chain in range(4):
        j, reverse = chain % 2, chain >= 2
        hi, mid, low = parts_of(log_decay[BLOCK * j : BLOCK * (j + 1)])
        tri = ones_where(upper if reverse else lower)
        cumulated = (dot(tri, hi) + dot(tri, mid) + dot(tri, low)) * LOG2E
        last = cumulated[0:1] if reverse else cumulated[BLOCK - 1 : BLOCK]
        if not reverse:
            lasts.append(jnp.exp2(last))
        cums[chain] = cumulated
        tails[chain] = split(jnp.exp2(last - cumulated))
        ecum[chain] = split(jnp.exp2(cumulated))
    top = iota((8, BLOCK), 0) == 0
    decays = jnp.where(top, lasts[0], lasts[1])
    decay_out[...] = decays
    decay_in[me] = decays

    def decay_copy(target, slot):
        return pltpu.make_async_remote_copy(
            src_ref=decay_out,
            dst_ref=decay_in.at[slot],
            send_sem=decay_send.at[target],
            recv_sem=decay_recv.at[slot],
            device_id={"seq": target},
            device_id_type=pl.DeviceIdType.MESH,
        )

    def pair_copy(j):
        return pltpu.make_async_remote_copy(
            src_ref=pair_out.at[2 * (1 - core) + j],
            dst_ref=pair_in.at[j],
            send_sem=pair_send.at[j],
            recv_sem=pair_recv.at[j],
            device_id={"seq": partner},
            device_id_type=pl.DeviceIdType.MESH,
        )

    def sum_copy(target, slot):
        return pltpu.make_async_remote_copy(
            src_ref=sum_out.at[target],
            dst_ref=sum_in.at[slot],
            send_sem=sum_send.at[target],
            recv_sem=sum_recv.at[slot],
            device_id={"seq": 2 * target + core},
            device_id_type=pl.DeviceIdType.MESH,
        )

    def mem_copy(target, slot):
        return pltpu.make_async_remote_copy(
            src_ref=mem_out.at[target],
            dst_ref=mem_in.at[slot],
            send_sem=mem_send.at[target],
            recv_sem=mem_recv.at[slot],
            device_id={"seq": 2 * target + core},
            device_id_type=pl.DeviceIdType.MESH,
        )

    def cross_copy(j):
        return pltpu.make_async_remote_copy(
            src_ref=cross_out.at[j],
            dst_ref=cross_in.at[j],
            send_sem=cross_send.at[j],
            recv_sem=cross_recv.at[j],
            device_id={"seq": partner},
            device_id_type=pl.DeviceIdType.MESH,
        )

    for k in range(1, COUNT):
        decay_copy(lax.rem(me + k, COUNT), me).start()

    loads[5].wait()
    for c in range(0, MIX, 384):
        cols = slice(c, c + 384)
        mixed = dot(normal[...], weight[:, E + c : E + c + 384]).astype(BF16).astype(F32)
        ext[0, HALO : HALO + BLOCK, cols] = mixed[:BLOCK]
        ext[1, HALO : HALO + BLOCK, cols] = mixed[BLOCK:]

    to_right.wait()
    to_left.wait()
    left_rows = jnp.where(me == 0, 0.0, halo[0].astype(F32))
    right_rows = jnp.where(me == COUNT - 1, 0.0, halo[1].astype(F32))
    rim = jnp.concatenate([left_rows, right_rows], axis=0).astype(BF16)
    rim_normals = jnp.concatenate(normals(rim), axis=0)
    for c in range(0, MIX, 384):
        cols = slice(c, c + 384)
        mixed = dot(rim_normals, weight[:, E + c : E + c + 384]).astype(BF16).astype(F32)
        for j in range(2):
            ext[j, 0:HALO, cols] = mixed[2 * HALO * j : 2 * HALO * j + HALO]
            ext[j, HALO + BLOCK : 2 * HALO + BLOCK, cols] = mixed[
                2 * HALO * j + HALO : 2 * HALO * (j + 1)
            ]

    loads[6].wait()
    loads[7].wait()
    for c in range(MIX // 128):
        cols = slice(128 * c, 128 * c + 128)
        taps = [conv_weight[k : k + 1, cols] for k in range(K)]
        start = conv_bias[cols][None, :]
        for j in range(2):
            views = [ext[j, HALO - 3 + r : HALO - 3 + r + BLOCK, cols] for r in range(7)]
            ahead = start
            behind = start
            for k in range(K):
                ahead = ahead + taps[k] * views[k]
                behind = behind + taps[k] * views[6 - k]
            act[j, :, cols] = silu(ahead).astype(BF16)
            act[2 + j, :, cols] = silu(behind).astype(BF16)

    for chain, j in [(2 * (1 - core) + j, j) for j in range(2)] + [(2 * core + j, None) for j in range(2)]:
        both = act[chain, :, E:]
        for c in range(0, E, 256):
            cols = slice(c, c + 256)
            factor = dot(tails[chain], expand64[:, cols])
            decayed = (factor * act[chain, :, cols].astype(F32)).astype(BF16)
            state = lax.dot_general(
                both, decayed, (((0,), (0,)), ((), ())), preferred_element_type=F32
            )
            pair_out[chain, :, cols] = state[:N].astype(BF16)
        if j is not None:
            pair_copy(j).start()

    for k in range(1, COUNT):
        other = lax.rem(me + k, COUNT)
        decay_copy(other, other).wait()
    near = [dot(split(decay_in[d]), expand64[...]) for d in (me, partner)]
    for j in range(2):
        pair_copy(j).wait()
        joined = near[1][j : j + 1] * pair_out[2 * core + j].astype(F32) + pair_in[j].astype(F32)
        joined = joined.astype(BF16)
        for q in range(4):
            sum_out[4 * j + q] = joined[16 * q : 16 * q + 16]
        for q in range(4):
            target = 4 * j + lax.rem(chip + q, 4)

            @pl.when(target != chip)
            def _():
                sum_copy(target, chip).start()
    sum_in[chip] = sum_out[chip]

    loads[8].wait()
    for c in range(0, E, 256):
        cols = slice(c, c + 256)
        gate = dot(normal[...], weight[:, cols]).astype(BF16).astype(F32)
        silu_gate[:, cols] = silu(gate)
    loads[9].wait()
    loads[10].wait()
    loads[11].wait()
    for r in range(0, E, 256):
        out_flipped[r : r + 256, :] = dot(out_weight[r : r + 256, :], flip).astype(BF16)
    repeat = ones_where(iota((HEADS, E), 1) // 64 == iota((HEADS, E), 0))
    skip = exact(jnp.broadcast_to(skip_gain[...], (8, HEADS)), repeat)[0:1]
    first = ones_where(iota(square, 1) < 64)
    second = ones_where(iota(square, 1) >= 64)
    for chain in range(4):
        reverse = chain >= 2
        columns = split(cums[chain])
        by_head = cums[chain].T
        both = act[chain, :, E:]
        reader = dot(both, shift).astype(BF16)
        scores = lax.dot_general(
            reader, both, (((1,), (1,)), ((), ())), preferred_element_type=F32
        )
        scores = jnp.where(upper if reverse else lower, scores, 0.0)
        scores = jnp.concatenate([scores, scores], axis=1)
        for p in range(HEADS // 2):
            cols = slice(128 * p, 128 * p + 128)
            at = dot(columns, expand128[:, 256 * p : 256 * p + 256])
            since = jnp.concatenate(
                [by_head[2 * p : 2 * p + 1], by_head[2 * p + 1 : 2 * p + 2]], axis=1
            )
            weights = (jnp.exp2(jnp.minimum(at - since, 0.0)) * scores).astype(BF16)
            signal = act[chain, :, cols]
            pair = jnp.concatenate([signal * first, signal * second], axis=0)
            inside[chain, :, cols] = dot(weights, pair) + skip[:, cols] * signal.astype(F32)

    mine = jnp.where(chip < 4, decay_in[:, 0, :], decay_in[:, 1, :])
    spread = dot(split(mine), expand64[...])
    carry = jnp.zeros((16, E), F32)
    for k in range(COUNT // 2):
        back = COUNT // 2 - 1 - k
        source = jnp.where(core == 0, k, back)
        mem_out[source] = carry.astype(BF16)

        @pl.when(source != chip)
        def _():
            sum_copy(source, source).wait()
            mem_copy(source, chip).start()

        factor = jnp.where(
            core == 0,
            spread[2 * k : 2 * k + 1] * spread[2 * k + 1 : 2 * k + 2],
            spread[2 * back : 2 * back + 1] * spread[2 * back + 1 : 2 * back + 2],
        )
        carry = factor * carry + sum_in[source].astype(F32)
    mem_in[chip] = mem_out[chip]

    def finish(chain, j, memory):
        reader = dot(act[chain, :, E:], shift).astype(BF16)[:, :N]
        total = jnp.zeros((BLOCK, 1), F32)
        for c in range(0, E, 256):
            cols = slice(c, c + 256)
            carried = dot(reader, memory[:, cols])
            scale = dot(ecum[chain], expand64[:, cols])
            gated = (inside[chain, :, cols] + scale * carried) * silu_gate[
                BLOCK * j : BLOCK * (j + 1), cols
            ]
            total = total + jnp.sum(gated * gated, axis=1, keepdims=True)
            inside[chain, :, cols] = gated
        scale = lax.rsqrt(total / E + EPS)
        final = (inside[chain] * scale * gate_gain[...]).astype(BF16)
        return dot(final, out_weight[...] if j == 0 else out_flipped[...])

    memories = []
    for j in range(2):
        for q in range(4):
            owner = 4 * j + q

            @pl.when(owner != chip)
            def _():
                mem_copy(owner, owner).wait()

        memory = jnp.concatenate([mem_in[4 * j + q] for q in range(4)], axis=0)
        onward = near[0][j : j + 1] * memory.astype(F32) + pair_out[2 * core + j].astype(F32)
        cross_out[j] = onward.astype(BF16)
        cross_copy(j).start()
        memories.append(memory)
    own = finish(2 * core, 0, memories[0]) + finish(2 * core + 1, 1, memories[1])
    other = jnp.zeros((BLOCK, D), F32)
    for j in range(2):
        cross_copy(j).wait()
        other = other + finish(2 * (1 - core) + j, j, cross_in[j])
    forward = jnp.where(core == 0, own, other)
    backward = jnp.where(core == 0, other, own).astype(BF16).astype(F32)
    out[...] = (forward + backward).astype(BF16)


def on_device(
    hidden,
    norm_gain,
    input_weight,
    step_weight,
    conv_weight,
    conv_bias,
    step_bias,
    log_rate,
    skip_gain,
    gate_gain,
    output_weight,
):
    vmem = pl.BlockSpec(memory_space=pltpu.VMEM)
    dma = pltpu.SemaphoreType.DMA
    return pl.pallas_call(
        kernel,
        out_shape=jax.ShapeDtypeStruct((BLOCK, D), BF16),
        in_specs=[pl.BlockSpec(memory_space=pltpu.HBM)] * 11,
        out_specs=vmem,
        scratch_shapes=[
            pltpu.VMEM((BLOCK, D), BF16),
            pltpu.VMEM((1, D), F32),
            pltpu.VMEM((HEADS, D), BF16),
            pltpu.VMEM((K, MIX), F32),
            pltpu.VMEM((MIX,), F32),
            pltpu.VMEM((1, HEADS), F32),
            pltpu.VMEM((1, HEADS), F32),
            pltpu.VMEM((1, HEADS), F32),
            pltpu.VMEM((1, E), F32),
            pltpu.VMEM((D, E + MIX), BF16),
            pltpu.VMEM((E, D), BF16),
            pltpu.VMEM((E, D), BF16),
            pltpu.VMEM((2, HALO, D), BF16),
            pltpu.VMEM((2 * BLOCK, D), BF16),
            pltpu.VMEM((2, BLOCK + 2 * HALO, MIX), F32),
            pltpu.VMEM((4, BLOCK, MIX), BF16),
            pltpu.VMEM((2 * BLOCK, E), F32),
            pltpu.VMEM((4, BLOCK, E), F32),
            pltpu.VMEM((4, BLOCK, BLOCK), BF16),
            pltpu.VMEM((4, BLOCK, BLOCK), BF16),
            pltpu.VMEM((4, BLOCK, BLOCK), F32),
            pltpu.VMEM((4, N, E), BF16),
            pltpu.VMEM((2, N, E), BF16),
            pltpu.VMEM((8, BLOCK), F32),
            pltpu.VMEM((COUNT, 8, BLOCK), F32),
            pltpu.VMEM((COUNT // 2, 16, E), BF16),
            pltpu.VMEM((COUNT // 2, 16, E), BF16),
            pltpu.VMEM((COUNT // 2, 16, E), BF16),
            pltpu.VMEM((COUNT // 2, 16, E), BF16),
            pltpu.VMEM((2, N, E), BF16),
            pltpu.VMEM((2, N, E), BF16),
            pltpu.VMEM((BLOCK, E), BF16),
            pltpu.VMEM((BLOCK, HEADS * BLOCK), BF16),
            dma((12,)),
            dma((2,)),
            dma((2,)),
            dma((COUNT,)),
            dma((COUNT,)),
            dma((2,)),
            dma((2,)),
            dma((COUNT // 2,)),
            dma((COUNT // 2,)),
            dma((COUNT // 2,)),
            dma((COUNT // 2,)),
            dma((2,)),
            dma((2,)),
        ],
        compiler_params=pltpu.CompilerParams(
            collective_id=0, has_side_effects=True, vmem_limit_bytes=32 * 1024 * 1024
        ),
    )(
        hidden,
        norm_gain[None],
        input_weight,
        step_weight.T,
        conv_weight,
        conv_bias,
        step_bias[None],
        log_rate[None],
        skip_gain[None],
        gate_gain[None],
        output_weight,
    )


def solution(mesh):
    in_specs = (P(("batch", "seq"), None), P(), P(), P(), P(), P(), P(), P(), P(), P(), P())
    out_specs = P(("batch", "seq"), None)
    return jax.shard_map(
        on_device, mesh=mesh, in_specs=in_specs, out_specs=out_specs, check_vma=False
    )
```

```python
import jax
import jax.numpy as jnp
from jax import lax
from jax.experimental import pallas as pl
from jax.experimental.pallas import tpu as pltpu
from jax.sharding import PartitionSpec as P

D = 512
E = 1024
N = 64
K = 4
BLOCK = 128
HEADS = 16
MIX = E + 2 * N
COUNT = 16
HALO = 16
EPS = 1e-05
LOG2E = 1.4426950408889634

F32 = jnp.float32
BF16 = jnp.bfloat16


def dot(a, b):
    return jnp.dot(a, b, preferred_element_type=F32)


def iota(shape, dim):
    return lax.broadcasted_iota(jnp.int32, shape, dim)


def ones_where(mask):
    return jnp.where(mask, 1.0, 0.0).astype(BF16)


def parts_of(x):
    hi = x.astype(BF16)
    rest = x - hi.astype(F32)
    mid = rest.astype(BF16)
    low = (rest - mid.astype(F32)).astype(BF16)
    return hi, mid, low


def split(x):
    hi, mid, low = parts_of(x)
    group = iota(x.shape, 1) // HEADS
    picked = jnp.where(
        group == 0,
        hi.astype(F32),
        jnp.where(group == 1, mid.astype(F32), jnp.where(group == 2, low.astype(F32), 0.0)),
    )
    return picked.astype(BF16)


def exact(values, ones):
    hi, mid, low = parts_of(values)
    return dot(hi, ones) + dot(mid, ones) + dot(low, ones)


def silu(x):
    return x / (1.0 + jnp.exp(-x))


def kernel(
    hidden_hbm,
    norm_gain_hbm,
    weight_hbm,
    step_weight_hbm,
    conv_weight_hbm,
    conv_bias_hbm,
    step_bias_hbm,
    log_rate_hbm,
    skip_gain_hbm,
    gate_gain_hbm,
    out_weight_hbm,
    out,
    hidden,
    norm_gain,
    step_weight,
    conv_weight,
    conv_bias,
    step_bias,
    log_rate,
    skip_gain,
    gate_gain,
    weight,
    out_weight,
    out_flipped,
    halo,
    normal,
    ext,
    act,
    silu_gate,
    inside,
    factors,
    readers,
    ecum,
    tails,
    cums,
    pair_out,
    pair_in,
    decay_out,
    decay_in,
    sum_out,
    sum_in,
    mem_out,
    mem_in,
    cross_out,
    cross_in,
    expand64,
    expand128,
    load_sem,
    halo_send,
    halo_recv,
    decay_send,
    decay_recv,
    pair_send,
    pair_recv,
    sum_send,
    sum_recv,
    mem_send,
    mem_recv,
    cross_send,
    cross_recv,
):
    me = lax.axis_index("seq")
    chip, core = me // 2, lax.rem(me, 2)
    partner = me + 1 - 2 * core
    moves = [
        (hidden_hbm, hidden),
        (norm_gain_hbm, norm_gain),
        (step_weight_hbm, step_weight),
        (step_bias_hbm, step_bias),
        (log_rate_hbm, log_rate),
        (weight_hbm.at[:, pl.ds(E, MIX)], weight.at[:, pl.ds(E, MIX)]),
        (conv_weight_hbm, conv_weight),
        (conv_bias_hbm, conv_bias),
        (weight_hbm.at[:, pl.ds(0, E)], weight.at[:, pl.ds(0, E)]),
        (skip_gain_hbm, skip_gain),
        (out_weight_hbm, out_weight),
        (gate_gain_hbm, gate_gain),
    ]
    loads = [
        pltpu.make_async_copy(source, target, load_sem.at[i])
        for i, (source, target) in enumerate(moves)
    ]

    loads[0].start()
    barrier = pltpu.get_barrier_semaphore()
    for k in range(1, COUNT):
        pl.semaphore_signal(
            barrier,
            inc=1,
            device_id={"seq": lax.rem(me + k, COUNT)},
            device_id_type=pl.DeviceIdType.MESH,
        )
    for load in loads[1:]:
        load.start()

    flip = ones_where(iota((D, D), 0) + iota((D, D), 1) == D - 1)
    rows = iota((BLOCK, E), 0)
    expand64[...] = ones_where((rows % HEADS == iota((BLOCK, E), 1) // 64) & (rows < 3 * HEADS))
    wide = (BLOCK, HEADS * BLOCK)
    rows = iota(wide, 0)
    expand128[...] = ones_where((rows % HEADS == iota(wide, 1) // BLOCK) & (rows < 3 * HEADS))
    tile = ones_where(iota((HEADS, BLOCK), 1) % HEADS == iota((HEADS, BLOCK), 0))
    square = (BLOCK, BLOCK)
    lower = iota(square, 0) >= iota(square, 1)
    upper = iota(square, 0) <= iota(square, 1)
    shift = ones_where(iota(square, 0) == iota(square, 1) + N)
    loads[0].wait()
    pl.semaphore_wait(barrier, COUNT - 1)
    to_right = pltpu.make_async_remote_copy(
        src_ref=hidden.at[pl.ds(BLOCK - HALO, HALO)],
        dst_ref=halo.at[0],
        send_sem=halo_send.at[0],
        recv_sem=halo_recv.at[0],
        device_id={"seq": lax.rem(me + 1, COUNT)},
        device_id_type=pl.DeviceIdType.MESH,
    )
    to_left = pltpu.make_async_remote_copy(
        src_ref=hidden.at[pl.ds(0, HALO)],
        dst_ref=halo.at[1],
        send_sem=halo_send.at[1],
        recv_sem=halo_recv.at[1],
        device_id={"seq": lax.rem(me + COUNT - 1, COUNT)},
        device_id_type=pl.DeviceIdType.MESH,
    )
    to_right.start()
    to_left.start()

    loads[1].wait()
    gain = norm_gain[...]

    def normals(raw):
        floats = raw.astype(F32)
        scale = lax.rsqrt(jnp.mean(floats * floats, axis=-1, keepdims=True) + EPS)
        turned = dot(raw, flip)
        return (floats * scale * gain).astype(BF16), (turned * scale * gain).astype(BF16)

    straight, turned = normals(hidden[...])
    normal[0:BLOCK, :] = straight
    normal[BLOCK : 2 * BLOCK, :] = turned

    for load in loads[2:5]:
        load.wait()
    step_tiled = lax.dot_general(
        tile, step_weight[...], (((0,), (0,)), ((), ())), preferred_element_type=F32
    ).astype(BF16)
    bias = exact(jnp.broadcast_to(step_bias[...], (8, HEADS)), tile)[0:1]
    rate = jnp.exp(exact(jnp.broadcast_to(log_rate[...], (8, HEADS)), tile)[0:1])
    raw = bias + lax.dot_general(
        normal[...], step_tiled, (((1,), (1,)), ((), ())), preferred_element_type=F32
    )
    soft = jnp.maximum(raw, 0.0) + jnp.log1p(jnp.exp(-jnp.abs(raw)))
    log_decay = -rate * soft
    lasts = []
    for chain in range(4):
        j, reverse = chain % 2, chain >= 2
        hi, mid, low = parts_of(log_decay[BLOCK * j : BLOCK * (j + 1)])
        tri = ones_where(upper if reverse else lower)
        cumulated = (dot(tri, hi) + dot(tri, mid) + dot(tri, low)) * LOG2E
        last = cumulated[0:1] if reverse else cumulated[BLOCK - 1 : BLOCK]
        if not reverse:
            lasts.append(jnp.exp2(last))
        cums[chain] = cumulated
        tails[chain] = split(jnp.exp2(last - cumulated))
        ecum[chain] = split(jnp.exp2(cumulated))
    top = iota((8, BLOCK), 0) == 0
    decays = jnp.where(top, lasts[0], lasts[1])
    decay_out[...] = decays
    decay_in[me] = decays

    def decay_copy(target, slot):
        return pltpu.make_async_remote_copy(
            src_ref=decay_out,
            dst_ref=decay_in.at[slot],
            send_sem=decay_send.at[target],
            recv_sem=decay_recv.at[slot],
            device_id={"seq": target},
            device_id_type=pl.DeviceIdType.MESH,
        )

    def pair_copy(j):
        return pltpu.make_async_remote_copy(
            src_ref=pair_out.at[2 * (1 - core) + j],
            dst_ref=pair_in.at[j],
            send_sem=pair_send.at[j],
            recv_sem=pair_recv.at[j],
            device_id={"seq": partner},
            device_id_type=pl.DeviceIdType.MESH,
        )

    def sum_copy(target, slot):
        return pltpu.make_async_remote_copy(
            src_ref=sum_out.at[target],
            dst_ref=sum_in.at[slot],
            send_sem=sum_send.at[target],
            recv_sem=sum_recv.at[slot],
            device_id={"seq": 2 * target + core},
            device_id_type=pl.DeviceIdType.MESH,
        )

    def mem_copy(target, slot):
        return pltpu.make_async_remote_copy(
            src_ref=mem_out.at[target],
            dst_ref=mem_in.at[slot],
            send_sem=mem_send.at[target],
            recv_sem=mem_recv.at[slot],
            device_id={"seq": 2 * target + core},
            device_id_type=pl.DeviceIdType.MESH,
        )

    def cross_copy(j):
        return pltpu.make_async_remote_copy(
            src_ref=cross_out.at[j],
            dst_ref=cross_in.at[j],
            send_sem=cross_send.at[j],
            recv_sem=cross_recv.at[j],
            device_id={"seq": partner},
            device_id_type=pl.DeviceIdType.MESH,
        )

    for k in range(1, COUNT):
        decay_copy(lax.rem(me + k, COUNT), me).start()

    loads[5].wait()
    for c in range(0, MIX, 384):
        cols = slice(c, c + 384)
        mixed = dot(normal[...], weight[:, E + c : E + c + 384]).astype(BF16).astype(F32)
        ext[0, HALO : HALO + BLOCK, cols] = mixed[:BLOCK]
        ext[1, HALO : HALO + BLOCK, cols] = mixed[BLOCK:]

    to_right.wait()
    to_left.wait()
    left_rows = jnp.where(me == 0, 0.0, halo[0].astype(F32))
    right_rows = jnp.where(me == COUNT - 1, 0.0, halo[1].astype(F32))
    rim = jnp.concatenate([left_rows, right_rows], axis=0).astype(BF16)
    rim_normals = jnp.concatenate(normals(rim), axis=0)
    for c in range(0, MIX, 384):
        cols = slice(c, c + 384)
        mixed = dot(rim_normals, weight[:, E + c : E + c + 384]).astype(BF16).astype(F32)
        for j in range(2):
            ext[j, 0:HALO, cols] = mixed[2 * HALO * j : 2 * HALO * j + HALO]
            ext[j, HALO + BLOCK : 2 * HALO + BLOCK, cols] = mixed[
                2 * HALO * j + HALO : 2 * HALO * (j + 1)
            ]

    loads[6].wait()
    loads[7].wait()
    for c in range(MIX // 128):
        cols = slice(128 * c, 128 * c + 128)
        taps = [conv_weight[k : k + 1, cols] for k in range(K)]
        start = conv_bias[cols][None, :]
        for j in range(2):
            views = [ext[j, HALO - 3 + r : HALO - 3 + r + BLOCK, cols] for r in range(7)]
            ahead = start
            behind = start
            for k in range(K):
                ahead = ahead + taps[k] * views[k]
                behind = behind + taps[k] * views[6 - k]
            act[j, :, cols] = silu(ahead).astype(BF16)
            act[2 + j, :, cols] = silu(behind).astype(BF16)

    for chain, j in [(2 * (1 - core) + j, j) for j in range(2)] + [(2 * core + j, None) for j in range(2)]:
        both = act[chain, :, E:]
        for c in range(0, E, 256):
            cols = slice(c, c + 256)
            factor = dot(tails[chain], expand64[:, cols])
            decayed = (factor * act[chain, :, cols].astype(F32)).astype(BF16)
            state = lax.dot_general(
                both, decayed, (((0,), (0,)), ((), ())), preferred_element_type=F32
            )
            pair_out[chain, :, cols] = state[:N].astype(BF16)
        if j is not None:
            pair_copy(j).start()

    for k in range(1, COUNT):
        other = lax.rem(me + k, COUNT)
        decay_copy(other, other).wait()
    near = [dot(split(decay_in[d]), expand64[...]) for d in (me, partner)]
    for j in range(2):
        pair_copy(j).wait()
        joined = near[1][j : j + 1] * pair_out[2 * core + j].astype(F32) + pair_in[j].astype(F32)
        joined = joined.astype(BF16)
        for q in range(4):
            sum_out[4 * j + q] = joined[16 * q : 16 * q + 16]
        for q in range(4):
            target = 4 * j + lax.rem(chip + q, 4)

            @pl.when(target != chip)
            def _():
                sum_copy(target, chip).start()
    sum_in[chip] = sum_out[chip]

    loads[8].wait()
    for c in range(0, E, 256):
        cols = slice(c, c + 256)
        gate = dot(normal[...], weight[:, cols]).astype(BF16).astype(F32)
        silu_gate[:, cols] = silu(gate)
    loads[9].wait()
    loads[10].wait()
    loads[11].wait()
    for r in range(0, E, 256):
        out_flipped[r : r + 256, :] = dot(out_weight[r : r + 256, :], flip).astype(BF16)
    repeat = ones_where(iota((HEADS, E), 1) // 64 == iota((HEADS, E), 0))
    skip = exact(jnp.broadcast_to(skip_gain[...], (8, HEADS)), repeat)[0:1]
    first = ones_where(iota(square, 1) < 64)
    second = ones_where(iota(square, 1) >= 64)
    for chain in range(4):
        reverse = chain >= 2
        columns = split(cums[chain])
        by_head = cums[chain].T
        both = act[chain, :, E:]
        reader = dot(both, shift).astype(BF16)
        readers[chain] = reader
        gate_block = slice(BLOCK * (chain % 2), BLOCK * (chain % 2) + BLOCK)
        scores = lax.dot_general(
            reader, both, (((1,), (1,)), ((), ())), preferred_element_type=F32
        )
        scores = jnp.where(upper if reverse else lower, scores, 0.0)
        scores = jnp.concatenate([scores, scores], axis=1)
        for p in range(HEADS // 2):
            cols = slice(128 * p, 128 * p + 128)
            at = dot(columns, expand128[:, 256 * p : 256 * p + 256])
            since = jnp.concatenate(
                [by_head[2 * p : 2 * p + 1], by_head[2 * p + 1 : 2 * p + 2]], axis=1
            )
            weights = (jnp.exp2(jnp.minimum(at - since, 0.0)) * scores).astype(BF16)
            signal = act[chain, :, cols]
            pair = jnp.concatenate([signal * first, signal * second], axis=0)
            gate = silu_gate[gate_block, cols]
            local = dot(weights, pair) + skip[:, cols] * signal.astype(F32)
            inside[chain, :, cols] = local * gate
            factors[chain, :, cols] = dot(ecum[chain], expand64[:, cols]) * gate

    mine = jnp.where(chip < 4, decay_in[:, 0, :], decay_in[:, 1, :])
    spread = dot(split(mine), expand64[...])
    carry = jnp.zeros((16, E), F32)
    for k in range(COUNT // 2):
        back = COUNT // 2 - 1 - k
        source = jnp.where(core == 0, k, back)
        mem_out[source] = carry.astype(BF16)

        @pl.when(source != chip)
        def _():
            sum_copy(source, source).wait()
            mem_copy(source, chip).start()

        factor = jnp.where(
            core == 0,
            spread[2 * k : 2 * k + 1] * spread[2 * k + 1 : 2 * k + 2],
            spread[2 * back : 2 * back + 1] * spread[2 * back + 1 : 2 * back + 2],
        )
        carry = factor * carry + sum_in[source].astype(F32)
    mem_in[chip] = mem_out[chip]

    def finish(chain, j, memory):
        reader = readers[chain][:, :N]
        total = jnp.zeros((BLOCK, 1), F32)
        for c in range(0, E, 256):
            cols = slice(c, c + 256)
            carried = dot(reader, memory[:, cols])
            gated = inside[chain, :, cols] + factors[chain, :, cols] * carried
            total = total + jnp.sum(gated * gated, axis=1, keepdims=True)
            inside[chain, :, cols] = gated
        scale = lax.rsqrt(total / E + EPS)
        final = (inside[chain] * scale * gate_gain[...]).astype(BF16)
        return dot(final, out_weight[...] if j == 0 else out_flipped[...])

    memories = []
    for j in range(2):
        for q in range(4):
            owner = 4 * j + q

            @pl.when(owner != chip)
            def _():
                mem_copy(owner, owner).wait()

        memory = jnp.concatenate([mem_in[4 * j + q] for q in range(4)], axis=0)
        onward = near[0][j : j + 1] * memory.astype(F32) + pair_out[2 * core + j].astype(F32)
        cross_out[j] = onward.astype(BF16)
        cross_copy(j).start()
        memories.append(memory)
    own = finish(2 * core, 0, memories[0]) + finish(2 * core + 1, 1, memories[1])
    other = jnp.zeros((BLOCK, D), F32)
    for j in range(2):
        cross_copy(j).wait()
        other = other + finish(2 * (1 - core) + j, j, cross_in[j])
    forward = jnp.where(core == 0, own, other)
    backward = jnp.where(core == 0, other, own).astype(BF16).astype(F32)
    out[...] = (forward + backward).astype(BF16)


def on_device(
    hidden,
    norm_gain,
    input_weight,
    step_weight,
    conv_weight,
    conv_bias,
    step_bias,
    log_rate,
    skip_gain,
    gate_gain,
    output_weight,
):
    vmem = pl.BlockSpec(memory_space=pltpu.VMEM)
    dma = pltpu.SemaphoreType.DMA
    return pl.pallas_call(
        kernel,
        out_shape=jax.ShapeDtypeStruct((BLOCK, D), BF16),
        in_specs=[pl.BlockSpec(memory_space=pltpu.HBM)] * 11,
        out_specs=vmem,
        scratch_shapes=[
            pltpu.VMEM((BLOCK, D), BF16),
            pltpu.VMEM((1, D), F32),
            pltpu.VMEM((HEADS, D), BF16),
            pltpu.VMEM((K, MIX), F32),
            pltpu.VMEM((MIX,), F32),
            pltpu.VMEM((1, HEADS), F32),
            pltpu.VMEM((1, HEADS), F32),
            pltpu.VMEM((1, HEADS), F32),
            pltpu.VMEM((1, E), F32),
            pltpu.VMEM((D, E + MIX), BF16),
            pltpu.VMEM((E, D), BF16),
            pltpu.VMEM((E, D), BF16),
            pltpu.VMEM((2, HALO, D), BF16),
            pltpu.VMEM((2 * BLOCK, D), BF16),
            pltpu.VMEM((2, BLOCK + 2 * HALO, MIX), F32),
            pltpu.VMEM((4, BLOCK, MIX), BF16),
            pltpu.VMEM((2 * BLOCK, E), F32),
            pltpu.VMEM((4, BLOCK, E), F32),
            pltpu.VMEM((4, BLOCK, E), F32),
            pltpu.VMEM((4, BLOCK, BLOCK), BF16),
            pltpu.VMEM((4, BLOCK, BLOCK), BF16),
            pltpu.VMEM((4, BLOCK, BLOCK), BF16),
            pltpu.VMEM((4, BLOCK, BLOCK), F32),
            pltpu.VMEM((4, N, E), BF16),
            pltpu.VMEM((2, N, E), BF16),
            pltpu.VMEM((8, BLOCK), F32),
            pltpu.VMEM((COUNT, 8, BLOCK), F32),
            pltpu.VMEM((COUNT // 2, 16, E), BF16),
            pltpu.VMEM((COUNT // 2, 16, E), BF16),
            pltpu.VMEM((COUNT // 2, 16, E), BF16),
            pltpu.VMEM((COUNT // 2, 16, E), BF16),
            pltpu.VMEM((2, N, E), BF16),
            pltpu.VMEM((2, N, E), BF16),
            pltpu.VMEM((BLOCK, E), BF16),
            pltpu.VMEM((BLOCK, HEADS * BLOCK), BF16),
            dma((12,)),
            dma((2,)),
            dma((2,)),
            dma((COUNT,)),
            dma((COUNT,)),
            dma((2,)),
            dma((2,)),
            dma((COUNT // 2,)),
            dma((COUNT // 2,)),
            dma((COUNT // 2,)),
            dma((COUNT // 2,)),
            dma((2,)),
            dma((2,)),
        ],
        compiler_params=pltpu.CompilerParams(
            collective_id=0, has_side_effects=True, vmem_limit_bytes=60 * 1024 * 1024
        ),
    )(
        hidden,
        norm_gain[None],
        input_weight,
        step_weight.T,
        conv_weight,
        conv_bias,
        step_bias[None],
        log_rate[None],
        skip_gain[None],
        gate_gain[None],
        output_weight,
    )


def solution(mesh):
    in_specs = (P(("batch", "seq"), None), P(), P(), P(), P(), P(), P(), P(), P(), P(), P())
    out_specs = P(("batch", "seq"), None)
    return jax.shard_map(
        on_device, mesh=mesh, in_specs=in_specs, out_specs=out_specs, check_vma=False
    )
```

```python
import jax
import jax.numpy as jnp
from jax import lax
from jax.experimental import pallas as pl
from jax.experimental.pallas import tpu as pltpu
from jax.sharding import PartitionSpec as P

D = 512
E = 1024
N = 64
K = 4
BLOCK = 128
HEADS = 16
MIX = E + 2 * N
COUNT = 16
HALO = 16
EPS = 1e-05
LOG2E = 1.4426950408889634

F32 = jnp.float32
BF16 = jnp.bfloat16


def dot(a, b):
    return jnp.dot(a, b, preferred_element_type=F32)


def iota(shape, dim):
    return lax.broadcasted_iota(jnp.int32, shape, dim)


def ones_where(mask):
    return jnp.where(mask, 1.0, 0.0).astype(BF16)


def parts_of(x):
    hi = x.astype(BF16)
    rest = x - hi.astype(F32)
    mid = rest.astype(BF16)
    low = (rest - mid.astype(F32)).astype(BF16)
    return hi, mid, low


def split(x):
    hi, mid, low = parts_of(x)
    group = iota(x.shape, 1) // HEADS
    picked = jnp.where(
        group == 0,
        hi.astype(F32),
        jnp.where(group == 1, mid.astype(F32), jnp.where(group == 2, low.astype(F32), 0.0)),
    )
    return picked.astype(BF16)


def exact(values, ones):
    hi, mid, low = parts_of(values)
    return dot(hi, ones) + dot(mid, ones) + dot(low, ones)


def silu(x):
    return x / (1.0 + jnp.exp(-x))


def kernel(
    hidden_hbm,
    norm_gain_hbm,
    weight_hbm,
    step_weight_hbm,
    conv_weight_hbm,
    conv_bias_hbm,
    step_bias_hbm,
    log_rate_hbm,
    skip_gain_hbm,
    gate_gain_hbm,
    out_weight_hbm,
    out,
    hidden,
    norm_gain,
    step_weight,
    conv_weight,
    conv_bias,
    step_bias,
    log_rate,
    skip_gain,
    gate_gain,
    weight,
    out_weight,
    out_flipped,
    halo,
    normal,
    ext,
    act,
    silu_gate,
    inside,
    factors,
    readers,
    ecum,
    tails,
    cums,
    pair_out,
    pair_in,
    decay_out,
    decay_in,
    sum_out,
    sum_in,
    mem_out,
    mem_in,
    cross_out,
    cross_in,
    expand64,
    expand128,
    load_sem,
    halo_send,
    halo_recv,
    decay_send,
    decay_recv,
    pair_send,
    pair_recv,
    sum_send,
    sum_recv,
    mem_send,
    mem_recv,
    cross_send,
    cross_recv,
):
    me = lax.axis_index("seq")
    chip, core = me // 2, lax.rem(me, 2)
    partner = me + 1 - 2 * core
    moves = [
        (hidden_hbm, hidden),
        (norm_gain_hbm, norm_gain),
        (step_weight_hbm, step_weight),
        (step_bias_hbm, step_bias),
        (log_rate_hbm, log_rate),
        (weight_hbm.at[:, pl.ds(E, MIX)], weight.at[:, pl.ds(E, MIX)]),
        (conv_weight_hbm, conv_weight),
        (conv_bias_hbm, conv_bias),
        (weight_hbm.at[:, pl.ds(0, E)], weight.at[:, pl.ds(0, E)]),
        (skip_gain_hbm, skip_gain),
        (out_weight_hbm, out_weight),
        (gate_gain_hbm, gate_gain),
    ]
    loads = [
        pltpu.make_async_copy(source, target, load_sem.at[i])
        for i, (source, target) in enumerate(moves)
    ]

    loads[0].start()
    barrier = pltpu.get_barrier_semaphore()
    for k in range(1, COUNT):
        pl.semaphore_signal(
            barrier,
            inc=1,
            device_id={"seq": lax.rem(me + k, COUNT)},
            device_id_type=pl.DeviceIdType.MESH,
        )
    for load in loads[1:]:
        load.start()

    flip = ones_where(iota((D, D), 0) + iota((D, D), 1) == D - 1)
    rows = iota((BLOCK, E), 0)
    expand64[...] = ones_where((rows % HEADS == iota((BLOCK, E), 1) // 64) & (rows < 3 * HEADS))
    wide = (BLOCK, HEADS * BLOCK)
    rows = iota(wide, 0)
    expand128[...] = ones_where((rows % HEADS == iota(wide, 1) // BLOCK) & (rows < 3 * HEADS))
    tile = ones_where(iota((HEADS, BLOCK), 1) % HEADS == iota((HEADS, BLOCK), 0))
    square = (BLOCK, BLOCK)
    lower = iota(square, 0) >= iota(square, 1)
    upper = iota(square, 0) <= iota(square, 1)
    shift = ones_where(iota(square, 0) == iota(square, 1) + N)
    loads[0].wait()
    pl.semaphore_wait(barrier, COUNT - 1)
    to_right = pltpu.make_async_remote_copy(
        src_ref=hidden.at[pl.ds(BLOCK - HALO, HALO)],
        dst_ref=halo.at[0],
        send_sem=halo_send.at[0],
        recv_sem=halo_recv.at[0],
        device_id={"seq": lax.rem(me + 1, COUNT)},
        device_id_type=pl.DeviceIdType.MESH,
    )
    to_left = pltpu.make_async_remote_copy(
        src_ref=hidden.at[pl.ds(0, HALO)],
        dst_ref=halo.at[1],
        send_sem=halo_send.at[1],
        recv_sem=halo_recv.at[1],
        device_id={"seq": lax.rem(me + COUNT - 1, COUNT)},
        device_id_type=pl.DeviceIdType.MESH,
    )
    to_right.start()
    to_left.start()

    loads[1].wait()
    gain = norm_gain[...]

    def normals(raw):
        floats = raw.astype(F32)
        scale = lax.rsqrt(jnp.mean(floats * floats, axis=-1, keepdims=True) + EPS)
        turned = dot(raw, flip)
        return (floats * scale * gain).astype(BF16), (turned * scale * gain).astype(BF16)

    straight, turned = normals(hidden[...])
    normal[0:BLOCK, :] = straight
    normal[BLOCK : 2 * BLOCK, :] = turned

    for load in loads[2:5]:
        load.wait()
    step_tiled = lax.dot_general(
        tile, step_weight[...], (((0,), (0,)), ((), ())), preferred_element_type=F32
    ).astype(BF16)
    bias = exact(jnp.broadcast_to(step_bias[...], (8, HEADS)), tile)[0:1]
    rate = jnp.exp(exact(jnp.broadcast_to(log_rate[...], (8, HEADS)), tile)[0:1])
    raw = bias + lax.dot_general(
        normal[...], step_tiled, (((1,), (1,)), ((), ())), preferred_element_type=F32
    )
    soft = jnp.maximum(raw, 0.0) + jnp.log1p(jnp.exp(-jnp.abs(raw)))
    log_decay = -rate * soft
    lasts = []
    for chain in range(4):
        j, reverse = chain % 2, chain >= 2
        hi, mid, low = parts_of(log_decay[BLOCK * j : BLOCK * (j + 1)])
        tri = ones_where(upper if reverse else lower)
        cumulated = (dot(tri, hi) + dot(tri, mid) + dot(tri, low)) * LOG2E
        last = cumulated[0:1] if reverse else cumulated[BLOCK - 1 : BLOCK]
        if not reverse:
            lasts.append(jnp.exp2(last))
        cums[chain] = cumulated
        tails[chain] = split(jnp.exp2(last - cumulated))
        ecum[chain] = split(jnp.exp2(cumulated))
    top = iota((8, BLOCK), 0) == 0
    decays = jnp.where(top, lasts[0], lasts[1])
    decay_out[...] = decays
    decay_in[me] = decays

    def decay_copy(target, slot):
        return pltpu.make_async_remote_copy(
            src_ref=decay_out,
            dst_ref=decay_in.at[slot],
            send_sem=decay_send.at[target],
            recv_sem=decay_recv.at[slot],
            device_id={"seq": target},
            device_id_type=pl.DeviceIdType.MESH,
        )

    def pair_copy(j):
        return pltpu.make_async_remote_copy(
            src_ref=pair_out.at[2 * (1 - core) + j],
            dst_ref=pair_in.at[j],
            send_sem=pair_send.at[j],
            recv_sem=pair_recv.at[j],
            device_id={"seq": partner},
            device_id_type=pl.DeviceIdType.MESH,
        )

    def sum_copy(target, slot):
        return pltpu.make_async_remote_copy(
            src_ref=sum_out.at[target],
            dst_ref=sum_in.at[slot],
            send_sem=sum_send.at[target],
            recv_sem=sum_recv.at[slot],
            device_id={"seq": 2 * target + core},
            device_id_type=pl.DeviceIdType.MESH,
        )

    def mem_copy(target, slot):
        return pltpu.make_async_remote_copy(
            src_ref=mem_out.at[target],
            dst_ref=mem_in.at[slot],
            send_sem=mem_send.at[target],
            recv_sem=mem_recv.at[slot],
            device_id={"seq": 2 * target + core},
            device_id_type=pl.DeviceIdType.MESH,
        )

    def cross_copy(j):
        return pltpu.make_async_remote_copy(
            src_ref=cross_out.at[j],
            dst_ref=cross_in.at[j],
            send_sem=cross_send.at[j],
            recv_sem=cross_recv.at[j],
            device_id={"seq": partner},
            device_id_type=pl.DeviceIdType.MESH,
        )

    for k in range(1, COUNT):
        decay_copy(lax.rem(me + k, COUNT), me).start()

    loads[5].wait()
    for c in range(0, MIX, 384):
        cols = slice(c, c + 384)
        mixed = dot(normal[...], weight[:, E + c : E + c + 384]).astype(BF16).astype(F32)
        ext[0, HALO : HALO + BLOCK, cols] = mixed[:BLOCK]
        ext[1, HALO : HALO + BLOCK, cols] = mixed[BLOCK:]

    to_right.wait()
    to_left.wait()
    left_rows = jnp.where(me == 0, 0.0, halo[0].astype(F32))
    right_rows = jnp.where(me == COUNT - 1, 0.0, halo[1].astype(F32))
    rim = jnp.concatenate([left_rows, right_rows], axis=0).astype(BF16)
    rim_normals = jnp.concatenate(normals(rim), axis=0)
    for c in range(0, MIX, 384):
        cols = slice(c, c + 384)
        mixed = dot(rim_normals, weight[:, E + c : E + c + 384]).astype(BF16).astype(F32)
        for j in range(2):
            ext[j, 0:HALO, cols] = mixed[2 * HALO * j : 2 * HALO * j + HALO]
            ext[j, HALO + BLOCK : 2 * HALO + BLOCK, cols] = mixed[
                2 * HALO * j + HALO : 2 * HALO * (j + 1)
            ]

    loads[6].wait()
    loads[7].wait()
    for c in range(MIX // 128):
        cols = slice(128 * c, 128 * c + 128)
        taps = [conv_weight[k : k + 1, cols] for k in range(K)]
        start = conv_bias[cols][None, :]
        for j in range(2):
            views = [ext[j, HALO - 3 + r : HALO - 3 + r + BLOCK, cols] for r in range(7)]
            ahead = start
            behind = start
            for k in range(K):
                ahead = ahead + taps[k] * views[k]
                behind = behind + taps[k] * views[6 - k]
            act[j, :, cols] = silu(ahead).astype(BF16)
            act[2 + j, :, cols] = silu(behind).astype(BF16)

    for chain, j in [(2 * (1 - core) + j, j) for j in range(2)] + [(2 * core + j, None) for j in range(2)]:
        both = act[chain, :, E:]
        for c in range(0, E, 256):
            cols = slice(c, c + 256)
            factor = dot(tails[chain], expand64[:, cols])
            decayed = (factor * act[chain, :, cols].astype(F32)).astype(BF16)
            state = lax.dot_general(
                both, decayed, (((0,), (0,)), ((), ())), preferred_element_type=F32
            )
            pair_out[chain, :, cols] = state[:N].astype(BF16)
        if j is not None:
            pair_copy(j).start()

    for k in range(1, COUNT):
        other = lax.rem(me + k, COUNT)
        decay_copy(other, other).wait()
    near = [dot(split(decay_in[d]), expand64[...]) for d in (me, partner)]
    for j in range(2):
        pair_copy(j).wait()
        joined = near[1][j : j + 1] * pair_out[2 * core + j].astype(F32) + pair_in[j].astype(F32)
        joined = joined.astype(BF16)
        for q in range(4):
            sum_out[2 * q + (q + j) % 2] = joined[16 * q : 16 * q + 16]
        for q in range(4):
            across = lax.rem(chip // 2 + q, 4)
            target = 2 * across + lax.rem(across + j, 2)

            @pl.when(target != chip)
            def _():
                sum_copy(target, chip).start()
    sum_in[chip] = sum_out[chip]

    loads[8].wait()
    for c in range(0, E, 256):
        cols = slice(c, c + 256)
        gate = dot(normal[...], weight[:, cols]).astype(BF16).astype(F32)
        silu_gate[:, cols] = silu(gate)
    loads[9].wait()
    loads[10].wait()
    loads[11].wait()
    for r in range(0, E, 256):
        out_flipped[r : r + 256, :] = dot(out_weight[r : r + 256, :], flip).astype(BF16)
    repeat = ones_where(iota((HEADS, E), 1) // 64 == iota((HEADS, E), 0))
    skip = exact(jnp.broadcast_to(skip_gain[...], (8, HEADS)), repeat)[0:1]
    first = ones_where(iota(square, 1) < 64)
    second = ones_where(iota(square, 1) >= 64)
    for chain in range(4):
        reverse = chain >= 2
        columns = split(cums[chain])
        by_head = cums[chain].T
        both = act[chain, :, E:]
        reader = dot(both, shift).astype(BF16)
        readers[chain] = reader
        gate_block = slice(BLOCK * (chain % 2), BLOCK * (chain % 2) + BLOCK)
        scores = lax.dot_general(
            reader, both, (((1,), (1,)), ((), ())), preferred_element_type=F32
        )
        scores = jnp.where(upper if reverse else lower, scores, 0.0)
        scores = jnp.concatenate([scores, scores], axis=1)
        for p in range(HEADS // 2):
            cols = slice(128 * p, 128 * p + 128)
            at = dot(columns, expand128[:, 256 * p : 256 * p + 256])
            since = jnp.concatenate(
                [by_head[2 * p : 2 * p + 1], by_head[2 * p + 1 : 2 * p + 2]], axis=1
            )
            weights = (jnp.exp2(jnp.minimum(at - since, 0.0)) * scores).astype(BF16)
            signal = act[chain, :, cols]
            pair = jnp.concatenate([signal * first, signal * second], axis=0)
            gate = silu_gate[gate_block, cols]
            local = dot(weights, pair) + skip[:, cols] * signal.astype(F32)
            inside[chain, :, cols] = local * gate
            factors[chain, :, cols] = dot(ecum[chain], expand64[:, cols]) * gate

    mine = jnp.where(lax.rem(chip // 2 + chip, 2) == 0, decay_in[:, 0, :], decay_in[:, 1, :])
    spread = dot(split(mine), expand64[...])
    carry = jnp.zeros((16, E), F32)
    for k in range(COUNT // 2):
        back = COUNT // 2 - 1 - k
        source = jnp.where(core == 0, k, back)
        mem_out[source] = carry.astype(BF16)

        @pl.when(source != chip)
        def _():
            sum_copy(source, source).wait()
            mem_copy(source, chip).start()

        factor = jnp.where(
            core == 0,
            spread[2 * k : 2 * k + 1] * spread[2 * k + 1 : 2 * k + 2],
            spread[2 * back : 2 * back + 1] * spread[2 * back + 1 : 2 * back + 2],
        )
        carry = factor * carry + sum_in[source].astype(F32)
    mem_in[chip] = mem_out[chip]

    def finish(chain, j, memory):
        reader = readers[chain][:, :N]
        total = jnp.zeros((BLOCK, 1), F32)
        for c in range(0, E, 256):
            cols = slice(c, c + 256)
            carried = dot(reader, memory[:, cols])
            gated = inside[chain, :, cols] + factors[chain, :, cols] * carried
            total = total + jnp.sum(gated * gated, axis=1, keepdims=True)
            inside[chain, :, cols] = gated
        scale = lax.rsqrt(total / E + EPS)
        final = (inside[chain] * scale * gate_gain[...]).astype(BF16)
        return dot(final, out_weight[...] if j == 0 else out_flipped[...])

    memories = []
    for j in range(2):
        for q in range(4):
            owner = 2 * q + (q + j) % 2

            @pl.when(owner != chip)
            def _():
                mem_copy(owner, owner).wait()

        memory = jnp.concatenate([mem_in[2 * q + (q + j) % 2] for q in range(4)], axis=0)
        onward = near[0][j : j + 1] * memory.astype(F32) + pair_out[2 * core + j].astype(F32)
        cross_out[j] = onward.astype(BF16)
        cross_copy(j).start()
        memories.append(memory)
    own = finish(2 * core, 0, memories[0]) + finish(2 * core + 1, 1, memories[1])
    other = jnp.zeros((BLOCK, D), F32)
    for j in range(2):
        cross_copy(j).wait()
        other = other + finish(2 * (1 - core) + j, j, cross_in[j])
    forward = jnp.where(core == 0, own, other)
    backward = jnp.where(core == 0, other, own).astype(BF16).astype(F32)
    out[...] = (forward + backward).astype(BF16)


def on_device(
    hidden,
    norm_gain,
    input_weight,
    step_weight,
    conv_weight,
    conv_bias,
    step_bias,
    log_rate,
    skip_gain,
    gate_gain,
    output_weight,
):
    vmem = pl.BlockSpec(memory_space=pltpu.VMEM)
    dma = pltpu.SemaphoreType.DMA
    return pl.pallas_call(
        kernel,
        out_shape=jax.ShapeDtypeStruct((BLOCK, D), BF16),
        in_specs=[pl.BlockSpec(memory_space=pltpu.HBM)] * 11,
        out_specs=vmem,
        scratch_shapes=[
            pltpu.VMEM((BLOCK, D), BF16),
            pltpu.VMEM((1, D), F32),
            pltpu.VMEM((HEADS, D), BF16),
            pltpu.VMEM((K, MIX), F32),
            pltpu.VMEM((MIX,), F32),
            pltpu.VMEM((1, HEADS), F32),
            pltpu.VMEM((1, HEADS), F32),
            pltpu.VMEM((1, HEADS), F32),
            pltpu.VMEM((1, E), F32),
            pltpu.VMEM((D, E + MIX), BF16),
            pltpu.VMEM((E, D), BF16),
            pltpu.VMEM((E, D), BF16),
            pltpu.VMEM((2, HALO, D), BF16),
            pltpu.VMEM((2 * BLOCK, D), BF16),
            pltpu.VMEM((2, BLOCK + 2 * HALO, MIX), F32),
            pltpu.VMEM((4, BLOCK, MIX), BF16),
            pltpu.VMEM((2 * BLOCK, E), F32),
            pltpu.VMEM((4, BLOCK, E), F32),
            pltpu.VMEM((4, BLOCK, E), F32),
            pltpu.VMEM((4, BLOCK, BLOCK), BF16),
            pltpu.VMEM((4, BLOCK, BLOCK), BF16),
            pltpu.VMEM((4, BLOCK, BLOCK), BF16),
            pltpu.VMEM((4, BLOCK, BLOCK), F32),
            pltpu.VMEM((4, N, E), BF16),
            pltpu.VMEM((2, N, E), BF16),
            pltpu.VMEM((8, BLOCK), F32),
            pltpu.VMEM((COUNT, 8, BLOCK), F32),
            pltpu.VMEM((COUNT // 2, 16, E), BF16),
            pltpu.VMEM((COUNT // 2, 16, E), BF16),
            pltpu.VMEM((COUNT // 2, 16, E), BF16),
            pltpu.VMEM((COUNT // 2, 16, E), BF16),
            pltpu.VMEM((2, N, E), BF16),
            pltpu.VMEM((2, N, E), BF16),
            pltpu.VMEM((BLOCK, E), BF16),
            pltpu.VMEM((BLOCK, HEADS * BLOCK), BF16),
            dma((12,)),
            dma((2,)),
            dma((2,)),
            dma((COUNT,)),
            dma((COUNT,)),
            dma((2,)),
            dma((2,)),
            dma((COUNT // 2,)),
            dma((COUNT // 2,)),
            dma((COUNT // 2,)),
            dma((COUNT // 2,)),
            dma((2,)),
            dma((2,)),
        ],
        compiler_params=pltpu.CompilerParams(
            collective_id=0, has_side_effects=True, vmem_limit_bytes=60 * 1024 * 1024
        ),
    )(
        hidden,
        norm_gain[None],
        input_weight,
        step_weight.T,
        conv_weight,
        conv_bias,
        step_bias[None],
        log_rate[None],
        skip_gain[None],
        gate_gain[None],
        output_weight,
    )


def solution(mesh):
    in_specs = (P(("batch", "seq"), None), P(), P(), P(), P(), P(), P(), P(), P(), P(), P())
    out_specs = P(("batch", "seq"), None)
    return jax.shard_map(
        on_device, mesh=mesh, in_specs=in_specs, out_specs=out_specs, check_vma=False
    )
```
